128 devices in a mesh: gx: 8 (over z, core), gy: 16 (over y, x).
Axes of the slice: x: 4, y: 4, z: 4, core: 2. Of those that a mesh axis runs over, the one named last changes fastest.
Arguments:
- a_vals: bfloat16 [1, 2048, 5, 128, 128], P(None, ('gx', 'gy')), may hold values from -1.796875 to 1.796875
- a_cols: int32 [1, 2048, 5], P(None, ('gx', 'gy')), may hold values from 0 to 2047, as said below
- p_vals: bfloat16 [1, 2048, 2, 128, 128], P(None, ('gx', 'gy')), may hold values from -0.5 to 0.5
- p_cols: int32 [1, 2048, 2], P(None, ('gx', 'gy')), may hold values from 0 to 511, as said below
- p2_vals: bfloat16 [1, 512, 2, 128, 128], P(None, ('gx', 'gy')), may hold values from -0.5 to 0.5
- p2_cols: int32 [1, 512, 2], P(None, ('gx', 'gy')), may hold values from 0 to 127, as said below
Outputs:
- coarse: bfloat16 [1, 512, 7, 128, 128], P(None, ('gx', 'gy'))
- coarsest: bfloat16 [1, 128, 7, 128, 128], P(None, ('gx', 'gy'))
The draws below stay inside these ranges and needn't reach their ends.
Inputs may be any that keep to these rules, and one draw needn't show every extreme that they name: In the fine row order a_cols[u, 0] = u, and a_cols[u, 1], .., a_cols[u, 4] are (u + d) mod 2048 for four different d among -3 .. -1 and 1 .. 3, in rising order of d. p_cols[u, 0] = u // 4, and p_cols[u, 1] is (u // 4 + 1) mod 512 or (u // 4 - 1) mod 512. p2_cols[J, 0] = J // 4, and p2_cols[J, 1] is (J // 4 + 1) mod 128 or (J // 4 - 1) mod 128.
All inputs are finite; a program needn't handle non-finite values.
Results may differ from the reference program's by a relative error of at most 0.0095.
Values may be sent and summed in bfloat16 or wider, within the bound.
No kernel may reach another device: no remote copies, remote signals or barrier semaphores. Data moves between devices by JAX's collectives and lax.ppermute only.
A program may use at most 64 MiB of HBM per device.

```python
import jax
import jax.numpy as jnp
import numpy as np
from jax import lax

BLK = 128
K = 5
KP = 2
KC = 7
HALF = 3
AGG = 4
AGG2 = 4
SUP = 16
RS = 1
DEVICES = 128


def kept_offsets():
    others = [-3, -2, -1, 1, 2, 3]
    kept_table = []
    for dropped_a in range(6):
        for dropped_b in range(dropped_a + 1, 6):
            kept_table.append([others[member] for member in range(6) if member != dropped_a and member != dropped_b])
    return np.array(kept_table, dtype=np.int32)


def coarse_pairs(key, nrows, group_size, ncoarse):
    row_ids = jnp.arange(nrows, dtype=jnp.int32)
    aggregate = row_ids // group_size
    direction = jax.random.randint(key, (nrows,), 0, 2, dtype=jnp.int32) * 2 - 1
    return jnp.stack([aggregate, (aggregate + direction) % ncoarse], axis=1)


def draw_a_cols(key, part):
    nfine = RS * DEVICES * SUP
    row_ids = jnp.arange(nfine, dtype=jnp.int32)
    choose_pair = jax.random.randint(jax.random.fold_in(key, 11), (nfine,), 0, 15, dtype=jnp.int32)
    kept_table = jnp.asarray(kept_offsets())
    offsets = kept_table[choose_pair]
    columns = jnp.concatenate([row_ids[:, None], (row_ids[:, None] + offsets) % nfine], axis=1)
    return columns.reshape(RS, DEVICES * SUP, K)


def draw_p_cols(key, part):
    pairs_drawn = coarse_pairs(jax.random.fold_in(key, 23), RS * DEVICES * SUP, AGG, RS * DEVICES * AGG2)
    return pairs_drawn.reshape(RS, DEVICES * SUP, KP)


def draw_p2_cols(key, part):
    pairs_drawn = coarse_pairs(jax.random.fold_in(key, 37), RS * DEVICES * AGG2, AGG2, RS * DEVICES)
    return pairs_drawn.reshape(RS, DEVICES * AGG2, KP)


def block_scale(key, extent, cuts, least, top_value):
    factor_of, own = 1.0, jax.random.fold_in(key, 6)
    for axis_at, blocks in cuts:
        steps = jnp.exp(jax.random.uniform(jax.random.fold_in(own, axis_at), (blocks,), jnp.float32, least / len(cuts), top_value / len(cuts)))
        factor_of = factor_of * jnp.repeat(steps, extent[axis_at] // blocks).reshape([-1 if axis == axis_at else 1 for axis in range(len(extent))])
    return factor_of


def scatter_about(own_key, extent, spread, limit, split=(), held_as=jnp.bfloat16):
    drawn = spread * jax.random.normal(own_key, extent, jnp.float32)
    if split:
        drawn = drawn * block_scale(own_key, extent, split, -0.22, 0.18)
    return jnp.clip(drawn, -limit, limit).astype(held_as)


def setup_inputs(seed: int = 0) -> dict:
    key_list = jax.random.split(jax.random.key(seed), 7)
    return {
        "a_vals": scatter_about(key_list[0], (RS, DEVICES * SUP, K, BLK, BLK), 0.3, 1.796875, ((1, 128),)),
        "a_cols": draw_a_cols(jax.random.fold_in(key_list[6], 71), 0),
        "p_vals": scatter_about(key_list[2], (RS, DEVICES * SUP, KP, BLK, BLK), BLK ** -0.5, 0.5, ((1, 128),)),
        "p_cols": draw_p_cols(jax.random.fold_in(key_list[6], 71), 0),
        "p2_vals": scatter_about(key_list[4], (RS, DEVICES * AGG2, KP, BLK, BLK), BLK ** -0.5, 0.5, ((1, 128),)),
        "p2_cols": draw_p2_cols(jax.random.fold_in(key_list[6], 71), 0),
    }


def coarse_matrix(a_vals, a_cols, p_vals, p_cols, group_size):
    nrows = a_vals.shape[0]
    ncoarse = nrows // group_size
    blocking = 64
    steps_count = nrows // blocking
    row_ids = jnp.arange(nrows, dtype=jnp.int32)

    def products_of(pieces):
        a_block, columns, indices = pieces
        p_block = p_vals[columns].astype(jnp.float32)
        p_index = p_cols[columns]
        slots = (p_index - (indices // group_size)[:, None, None] + 2) % ncoarse
        onehot = (slots[..., None] == jnp.arange(5, dtype=jnp.int32)).astype(jnp.float32)
        block_terms = jnp.einsum("ukij,ukbjl->ukbil", a_block.astype(jnp.float32), p_block)
        return jnp.einsum("ukbs,ukbil->usil", onehot, block_terms).astype(jnp.bfloat16)

    a_parts = a_vals.reshape((steps_count, blocking) + a_vals.shape[1:])
    col_parts = a_cols.reshape((steps_count, blocking) + a_cols.shape[1:])
    row_parts = row_ids.reshape(steps_count, blocking)
    products = lax.map(products_of, (a_parts, col_parts, row_parts))

    def accumulate(summed, pieces):
        ap_block, pv_block, pc_block, indices = pieces
        block_terms = jnp.einsum("uaij,usil->uasjl", pv_block.astype(jnp.float32), ap_block.astype(jnp.float32))
        target = (indices // group_size)[:, None, None] + jnp.arange(5, dtype=jnp.int32)[None, None, :] + 1 - pc_block[:, :, None]
        target = target % ncoarse
        rows_hit = jnp.broadcast_to(pc_block[:, :, None], target.shape)
        return summed.at[rows_hit, target].add(block_terms), None

    start = jnp.zeros((ncoarse, KC, BLK, BLK), jnp.float32)
    pv_parts = p_vals.reshape((steps_count, blocking) + p_vals.shape[1:])
    pc_parts = p_cols.reshape((steps_count, blocking) + p_cols.shape[1:])
    summed, unused = lax.scan(accumulate, start, (products, pv_parts, pc_parts, row_parts))
    return summed.astype(jnp.bfloat16)


def reference(a_vals, a_cols, p_vals, p_cols, p2_vals, p2_cols):
    nfine = a_vals.shape[0] * a_vals.shape[1]
    coarse = coarse_matrix(a_vals.reshape(nfine, K, BLK, BLK), a_cols.reshape(nfine, K), p_vals.reshape(nfine, KP, BLK, BLK), p_cols.reshape(nfine, KP), AGG)
    ncoarse = coarse.shape[0]
    band_cols = (jnp.arange(ncoarse, dtype=jnp.int32)[:, None] + jnp.arange(KC, dtype=jnp.int32)[None, :] - HALF) % ncoarse
    coarsest = coarse_matrix(coarse, band_cols, p2_vals.reshape(ncoarse, KP, BLK, BLK), p2_cols.reshape(ncoarse, KP), AGG2)
    return coarse.reshape(RS, DEVICES * AGG2, KC, BLK, BLK), coarsest.reshape(RS, DEVICES, KC, BLK, BLK)
```

```python
import jax
import jax.numpy as jnp
from jax import lax
from jax.experimental import pallas as pl
from jax.experimental.pallas import tpu as pltpu
from jax.sharding import PartitionSpec as P

B = 128
K = 5
KC = 7
ROWS = 16
CROWS = 4
BF = jnp.bfloat16
F32 = jnp.float32
PM = 6 * B + 16
QM = 4 * B + 16
AXES = ("gx", "gy")


def blk(i, n=1):
    return pl.ds(i * B, n * B)


def side_at(cols, r, ncoarse):
    return lax.rem(cols[r, 1] - cols[r, 0] + 1 + ncoarse, ncoarse) - 1


def dot(a, b):
    return jnp.dot(a, b, preferred_element_type=F32)


def dot_t(a, b):
    return lax.dot_general(a, b, (((0,), (0,)), ((), ())), preferred_element_type=F32)


def pack_kernel(ncoarse, ncoarsest, p_cols, p2_cols, p_hbm, p2_hbm, pa, pb, qa, qb, sems):
    odd = p2_cols[0, 0] % 2
    jobs = []
    for n, (dst, flip) in enumerate(((pa, 0), (pb, 1), (qa, 0), (qb, 1))):
        high = (odd == flip).astype(jnp.int32)
        if n < 2:
            start, rows, src, cols, ncols = high * (ROWS - 3), 3, p_hbm, p_cols, ncoarse
        else:
            start, rows, src, cols, ncols = high * (CROWS - 2), 2, p2_hbm, p2_cols, ncoarsest
        size = rows * 2 * B
        copy = pltpu.make_async_copy(
            src.at[pl.ds(pl.multiple_of(start * 2 * B, 2 * B), size)], dst.at[pl.ds(0, size)], sems.at[n]
        )
        copy.start()
        jobs.append((copy, dst, start, rows, cols, ncols, size))
    row = lax.broadcasted_iota(jnp.int32, (16, B), 0)
    for copy, dst, start, rows, cols, ncols, size in jobs:
        flags = jnp.zeros((16, B), F32)
        for r in range(rows):
            side = side_at(cols, start + r, ncols)
            flags = jnp.where(row == 2 * r, (side < 0).astype(F32), flags)
            flags = jnp.where(row == 2 * r + 1, (side > 0).astype(F32), flags)
        copy.wait()
        dst[pl.ds(size, 16), :] = flags.astype(BF)


def bands_of(p_ref, cols, rows, ncoarse):
    out = []
    for r in rows:
        side = side_at(cols, r, ncoarse)
        p0 = p_ref[blk(2 * r), :]
        p1 = p_ref[blk(2 * r + 1), :]
        zero = jnp.zeros_like(p1)
        out.append((jnp.where(side < 0, p1, zero), p0, jnp.where(side > 0, p1, zero)))
    return out


def halo_bands(low, high, is_low, rows, size):
    def pick(start, n):
        return jnp.where(is_low, low[pl.ds(start, n), :], high[pl.ds(start, n), :])

    flags = pick(size, 16).astype(F32)
    out = []
    for r in range(rows):
        p0 = pick(2 * r * B, B)
        p1 = pick((2 * r + 1) * B, B)
        lower = jnp.broadcast_to(flags[2 * r : 2 * r + 1, :], (B, B)).astype(BF)
        upper = jnp.broadcast_to(flags[2 * r + 1 : 2 * r + 2, :], (B, B)).astype(BF)
        out.append((p1 * lower, p0, p1 * upper))
    return out


def stack_bands(bands):
    return jnp.concatenate([jnp.concatenate(band, axis=1) for band in bands], axis=0)


def inner_kernel(nfine, ncoarse, a_cols, p_cols, a_ref, p_ref, acc_out, part_out, acc, prod):
    base = a_cols[0, 0]
    edge = {0: 0, 1: 1, 2: 2, 3: 3, 12: 4, 13: 5, 14: 6, 15: 7}
    for g in (0, 3, 1, 2):
        for r in range(4 * g, 4 * g + 4):
            acc[...] = jnp.zeros_like(acc)
            for k in range(K):
                shift = lax.rem(a_cols[r, k] - (base + r) + 3 + nfine, nfine) - 3
                v = r + shift
                inside = jnp.logical_and(v >= 0, v < ROWS)
                v = jnp.clip(v, 0, ROWS - 1)
                side = side_at(p_cols, v, ncoarse)
                slot0 = jnp.where(inside, v // 4 - g + 2, 6)
                slot1 = slot0 + side
                w0 = p_ref[pl.ds(pl.multiple_of(v * 2 * B, 2 * B), B), :]
                w1 = p_ref[pl.ds(pl.multiple_of(v * 2 * B + B, B), B), :]
                terms = dot(a_ref[blk(r * K + k), :], jnp.concatenate([w0, w1], axis=1))
                acc[slot0] += terms[:, :B]
                acc[slot1] += terms[:, B:]
            for s in range(5):
                if r in edge or r in (4, 5, 6, 7, 8, 9, 10, 11):
                    pass
                if g in (0, 3):
                    acc_out[4 * (g // 3) + r % 4, :, s * B : (s + 1) * B] = acc[s]
                else:
                    prod[blk(r - 4), s * B : (s + 1) * B] = acc[s].astype(BF)
    part_out[...] = jnp.zeros_like(part_out)
    for g in (1, 2):
        bands = stack_bands(bands_of(p_ref, p_cols, range(4 * g, 4 * g + 4), ncoarse))
        terms = dot_t(bands, prod[blk(4 * (g - 1), 4), :])
        for m in range(3):
            at = slice((g - 1) * B, (g + 4) * B)
            part_out[g - 1 + m, :, at] = part_out[g - 1 + m, :, at] + terms[m * B : (m + 1) * B, :]


def outer_kernel(
    nfine, ncoarse, ncoarsest, a_cols, p_cols, p2_cols, a_ref, p_ref, p2_ref, acc_in, part_in,
    pa, pb, qa, qb, coarse_out, rim_out, fine_out, ma, mb, na, nb, prod, part, cp,
):
    base = a_cols[0, 0]
    d = p2_cols[0, 0]
    even = d % 2 == 0
    for g in (0, 3):
        for m in range(4):
            for s in range(5):
                pass
    for side in (0, 1):
        first = 0 if side == 0 else ROWS - 3
        bands = stack_bands(
            halo_bands(pb, pa, even, 3, 6 * B) if side == 0 else halo_bands(pa, pb, even, 3, 6 * B)
        )
        rows = []
        for r in range(first, first + 3):
            line = []
            for h in range(3):
                v = h - 3 if side == 0 else ROWS + h
                want = v - r
                if abs(want) > 3:
                    line.append(jnp.zeros((B, B), BF))
                    continue
                at = jnp.int32(0)
                found = jnp.int32(0)
                for k in range(1, K):
                    shift = lax.rem(a_cols[r, k] - (base + r) + 3 + nfine, nfine) - 3
                    hit = (shift == want).astype(jnp.int32)
                    at = at + hit * k
                    found = found + hit
                block = a_ref[pl.ds(pl.multiple_of((r * K + at) * B, B), B), :]
                line.append(jnp.where(found > 0, block, jnp.zeros_like(block)))
            rows.append(jnp.concatenate(line, axis=1))
        terms = dot(jnp.concatenate(rows, axis=0), bands)
        for n in range(4):
            r = 4 * side + n
            q = n if side == 0 else n - 1
            for s in range(5):
                value = acc_in[r, :, s * B : (s + 1) * B]
                lane = s if side == 0 else s - 2
                if 0 <= lane < 3 and 0 <= q < 3:
                    value = value + terms[q * B : (q + 1) * B, lane * B : (lane + 1) * B]
                prod[blk(r), s * B : (s + 1) * B] = value.astype(BF)
    part[...] = jnp.zeros_like(part)
    for j in range(4):
        part[j + 1, :, B : 7 * B] = part_in[j]
    for g in (0, 3):
        bands = stack_bands(bands_of(p_ref, p_cols, range(4 * g, 4 * g + 4), ncoarse))
        terms = dot_t(bands, prod[blk(4 * (g // 3), 4), :])
        for m in range(3):
            at = slice(g * B, (g + 5) * B)
            part[g + m, :, at] = part[g + m, :, at] + terms[m * B : (m + 1) * B, :]
    for j in range(4):
        for t in range(KC):
            q = t + j - 1
            if 0 <= q < 8:
                coarse_out[blk(j * KC + t), :] = part[j + 1, :, q * B : (q + 1) * B].astype(BF)
            else:
                coarse_out[blk(j * KC + t), :] = jnp.zeros((B, B), BF)
    for t in range(5):
        rim_out[blk(t), :] = part[1, :, (t - 1) * B : t * B] if t > 0 else jnp.zeros((B, B), F32)
        q = t + 4
        rim_out[blk(5 + t), :] = part[4, :, q * B : (q + 1) * B] if q < 8 else jnp.zeros((B, B), F32)
    low = halo_bands(qb, qa, even, 2, 4 * B)
    high = halo_bands(qa, qb, even, 2, 4 * B)
    own = bands_of(p2_ref, p2_cols, range(4), ncoarsest)
    lines = part[...].astype(BF).reshape(6 * B, 8 * B)
    ta = dot(lines[0 : 4 * B, 0 : 2 * B], stack_bands(low))
    tb = dot(lines[:, 2 * B : 6 * B], stack_bands(own))
    tc = dot(lines[2 * B : 6 * B, 6 * B : 8 * B], stack_bands(high))
    for e in range(5):
        total = [None] * 6
        for i in range(6):
            pieces = []
            if e < 3 and i < 4:
                pieces.append(ta[i * B : (i + 1) * B, e * B : (e + 1) * B])
            if 1 <= e < 4:
                pieces.append(tb[i * B : (i + 1) * B, (e - 1) * B : e * B])
            if e >= 2 and i >= 2:
                pieces.append(tc[(i - 2) * B : (i - 1) * B, (e - 2) * B : (e - 1) * B])
            value = sum(pieces[1:], pieces[0]) if pieces else jnp.zeros((B, B), F32)
            cp[blk(i), e * B : (e + 1) * B] = value.astype(BF)
    gm = dot_t(stack_bands(low[1:2]), cp[blk(0), :])
    g0 = dot_t(stack_bands(own), cp[blk(1, 4), :])
    gp = dot_t(stack_bands(high[0:1]), cp[blk(5), :])

    def row(x, m):
        return x[m * B : (m + 1) * B, :]

    fine_out[...] = row(gm, 2) + row(g0, 1) + row(gp, 0)
    to_low = (row(gm, 1) + row(g0, 0)).astype(BF)
    to_high = (row(g0, 2) + row(gp, 1)).astype(BF)
    two_low = row(gm, 0).astype(BF)
    two_high = row(gp, 2).astype(BF)

    def put(dst, coarse_row, q0, fine):
        for t in range(5):
            dst[blk(t), :] = part[coarse_row, :, (q0 + t) * B : (q0 + t + 1) * B].astype(BF)
            dst[blk(5 + t), :] = fine[:, t * B : (t + 1) * B]

    def put2(dst, fine, e0):
        for t in range(4):
            dst[blk(t), :] = fine[:, (e0 + t) * B : (e0 + t + 1) * B]

    @pl.when(even)
    def _():
        put(mb, 0, 0, to_low)
        put(ma, 5, 3, to_high)

    @pl.when(jnp.logical_not(even))
    def _():
        put(ma, 0, 0, to_low)
        put(mb, 5, 3, to_high)

    even2 = (d // 2) % 2 == 0

    @pl.when(even2)
    def _():
        put2(nb, two_low, 0)
        put2(na, two_high, 1)

    @pl.when(jnp.logical_not(even2))
    def _():
        put2(na, two_low, 0)
        put2(nb, two_high, 1)


def last_kernel(p2_cols, coarse_in, rim, fine, ma, mb, na, nb, coarse_out, coarsest_out, rows, sems):
    d = p2_cols[0, 0]
    even = d % 2 == 0
    even2 = (d // 2) % 2 == 0

    def one(low, t):
        if low:
            return jnp.where(even, mb[blk(t), :], ma[blk(t), :]).astype(F32)
        return jnp.where(even, ma[blk(t), :], mb[blk(t), :]).astype(F32)

    def two(low, t):
        if low:
            return jnp.where(even2, nb[blk(t), :], na[blk(t), :]).astype(F32)
        return jnp.where(even2, na[blk(t), :], nb[blk(t), :]).astype(F32)

    for t in range(5):
        rows[blk(t), :] = (rim[blk(t), :] + one(True, t)).astype(BF)
        rows[blk(5 + t), :] = (rim[blk(5 + t), :] + one(False, t)).astype(BF)
    copies = [
        pltpu.make_async_copy(rows.at[blk(0, 5)], coarse_out.at[blk(0, 5)], sems.at[0]),
        pltpu.make_async_copy(rows.at[blk(5, 5)], coarse_out.at[blk(3 * KC + 2, 5)], sems.at[1]),
    ]
    for copy in copies:
        copy.start()
    for t in range(KC):
        value = jnp.zeros((B, B), F32)
        if 1 <= t < 6:
            value = value + fine[:, (t - 1) * B : t * B]
        if t < 5:
            value = value + one(True, 5 + t)
        if t >= 2:
            value = value + one(False, 5 + t - 2)
        if t < 4:
            value = value + two(True, t)
        if t >= 3:
            value = value + two(False, t - 3)
        coarsest_out[blk(t), :] = value.astype(BF)
    for copy in copies:
        copy.wait()


def call(kernel, ins, outs, args, scratch=(), cost=None, **kw):
    smem = pl.BlockSpec(memory_space=pltpu.SMEM)
    vmem = pl.BlockSpec(memory_space=pltpu.VMEM)
    anyspec = pl.BlockSpec(memory_space=pl.ANY)
    kinds = {"s": smem, "v": vmem, "a": anyspec}
    return pl.pallas_call(
        kernel,
        in_specs=[kinds[c] for c in ins],
        out_specs=tuple(kinds[c] for c, _, _ in outs),
        out_shape=tuple(jax.ShapeDtypeStruct(shape, dtype) for _, shape, dtype in outs),
        scratch_shapes=list(scratch),
        compiler_params=pltpu.CompilerParams(vmem_limit_bytes=40 * 1024 * 1024),
        cost_estimate=cost,
        **kw,
    )(*args)


def body(a_vals, a_cols, p_vals, p_cols, p2_vals, p2_cols):
    devices = lax.axis_size(AXES)
    nfine = ROWS * devices
    ncoarse = CROWS * devices
    a_cols = a_cols.reshape(ROWS, K)
    p_cols = p_cols.reshape(ROWS, 2)
    p2_cols = p2_cols.reshape(CROWS, 2)
    a = a_vals.reshape(ROWS * K * B, B)
    p = p_vals.reshape(ROWS * 2 * B, B)
    p2 = p2_vals.reshape(CROWS * 2 * B, B)
    swap_a = [(i, i ^ 1) for i in range(devices)]
    swap_b = [(i, (i + 1) % devices if i % 2 else (i - 1) % devices) for i in range(devices)]
    skip_a = [(i, i ^ 2) for i in range(devices)]
    skip_b = [(i, (i + 2) % devices if i & 2 else (i - 2) % devices) for i in range(devices)]

    def pack(*refs):
        pack_kernel(ncoarse, devices, *refs)

    pa, pb, qa, qb = call(
        pack,
        "ssaa",
        [("v", (PM, B), BF), ("v", (PM, B), BF), ("v", (QM, B), BF), ("v", (QM, B), BF)],
        (p_cols, p2_cols, p, p2),
        [pltpu.SemaphoreType.DMA((4,))],
    )
    pa = lax.ppermute(pa, AXES, swap_a)
    pb = lax.ppermute(pb, AXES, swap_b)
    qa = lax.ppermute(qa, AXES, swap_a)
    qb = lax.ppermute(qb, AXES, swap_b)

    def inner(*refs):
        inner_kernel(nfine, ncoarse, *refs)

    acc, part = call(
        inner,
        "ssvv",
        [("v", (8, B, 5 * B), F32), ("v", (4, B, 6 * B), F32)],
        (a_cols, p_cols, a, p),
        [pltpu.VMEM((8, B, B), F32), pltpu.VMEM((8 * B, 5 * B), BF)],
        pl.CostEstimate(flops=10**9, bytes_accessed=8 * 10**6, transcendentals=0),
    )

    def outer(*refs):
        outer_kernel(nfine, ncoarse, devices, *refs)

    coarse, rim, fine, ma, mb, na, nb = call(
        outer,
        "sssvvvvvvvvv",
        [
            ("v", (CROWS * KC * B, B), BF),
            ("v", (10 * B, B), F32),
            ("v", (B, 5 * B), F32),
            ("v", (10 * B, B), BF),
            ("v", (10 * B, B), BF),
            ("v", (4 * B, B), BF),
            ("v", (4 * B, B), BF),
        ],
        (a_cols, p_cols, p2_cols, a, p, p2, acc, part, pa, pb, qa, qb),
        [pltpu.VMEM((8 * B, 5 * B), BF), pltpu.VMEM((6, B, 8 * B), F32), pltpu.VMEM((6 * B, 5 * B), BF)],
        pl.CostEstimate(flops=2 * 10**9, bytes_accessed=8 * 10**6, transcendentals=0),
    )
    mb = lax.ppermute(mb, AXES, swap_b)
    nb = lax.ppermute(nb, AXES, skip_b)
    ma = lax.ppermute(ma, AXES, swap_a)
    na = lax.ppermute(na, AXES, skip_a)
    coarse, coarsest = call(
        last_kernel,
        "savvvvvv",
        [("a", (CROWS * KC * B, B), BF), ("v", (KC * B, B), BF)],
        (p2_cols, coarse, rim, fine, ma, mb, na, nb),
        [pltpu.VMEM((10 * B, B), BF), pltpu.SemaphoreType.DMA((2,))],
        input_output_aliases={1: 0},
    )
    return coarse.reshape(1, CROWS, KC, B, B), coarsest.reshape(1, 1, KC, B, B)


def solution(mesh):
    blocks = P(None, AXES, None, None, None)
    cols = P(None, AXES, None)
    return jax.shard_map(
        body,
        mesh=mesh,
        in_specs=(blocks, cols, blocks, cols, blocks, cols),
        out_specs=(blocks, blocks),
        check_vma=False,
    )
```

```python
import jax
import jax.numpy as jnp
from jax import lax
from jax.experimental import pallas as pl
from jax.experimental.pallas import tpu as pltpu
from jax.sharding import PartitionSpec as P

B = 128
K = 5
KC = 7
ROWS = 16
CROWS = 4
BF = jnp.bfloat16
F32 = jnp.float32
PM = 6 * B + 16
QM = 4 * B + 16
AXES = ("gx", "gy")


def blk(i, n=1):
    return pl.ds(i * B, n * B)


def side_at(cols, r, ncoarse):
    return lax.rem(cols[1, r] - cols[0, r] + 1 + ncoarse, ncoarse) - 1


def place():
    return lax.axis_index(AXES)


def dot(a, b):
    return jnp.dot(a, b, preferred_element_type=F32)


def dot_t(a, b):
    return lax.dot_general(a, b, (((0,), (0,)), ((), ())), preferred_element_type=F32)


def pack_kernel(ncoarse, ncoarsest, pc_hbm, qc_hbm, p_hbm, p2_hbm, pa, pb, qa, qb, p_cols, p2_cols, sems):
    odd = place() % 2
    cols_in = [pltpu.make_async_copy(x, y, sems.at[4 + n]) for n, (x, y) in enumerate(((pc_hbm, p_cols), (qc_hbm, p2_cols)))]
    for copy in cols_in:
        copy.start()
    jobs = []
    for n, (dst, flip) in enumerate(((pa, 0), (pb, 1), (qa, 0), (qb, 1))):
        high = (odd == flip).astype(jnp.int32)
        if n < 2:
            start, rows, src, cols, ncols = high * (ROWS - 3), 3, p_hbm, p_cols, ncoarse
        else:
            start, rows, src, cols, ncols = high * (CROWS - 2), 2, p2_hbm, p2_cols, ncoarsest
        size = rows * 2 * B
        copy = pltpu.make_async_copy(
            src.at[pl.ds(pl.multiple_of(start * 2 * B, 2 * B), size)], dst.at[pl.ds(0, size)], sems.at[n]
        )
        copy.start()
        jobs.append((copy, dst, start, rows, cols, ncols, size))
    row = lax.broadcasted_iota(jnp.int32, (16, B), 0)
    for copy in cols_in:
        copy.wait()
    for copy, dst, start, rows, cols, ncols, size in jobs:
        flags = jnp.zeros((16, B), F32)
        for r in range(rows):
            side = side_at(cols, start + r, ncols)
            flags = jnp.where(row == 2 * r, (side < 0).astype(F32), flags)
            flags = jnp.where(row == 2 * r + 1, (side > 0).astype(F32), flags)
        copy.wait()
        dst[pl.ds(size, 16), :] = flags.astype(BF)


def bands_of(p_ref, cols, rows, ncoarse):
    out = []
    for r in rows:
        side = side_at(cols, r, ncoarse)
        p0 = p_ref[blk(2 * r), :]
        p1 = p_ref[blk(2 * r + 1), :]
        zero = jnp.zeros_like(p1)
        out.append((jnp.where(side < 0, p1, zero), p0, jnp.where(side > 0, p1, zero)))
    return out


def halo_bands(low, high, is_low, rows, size):
    def pick(start, n):
        return jnp.where(is_low, low[pl.ds(start, n), :], high[pl.ds(start, n), :])

    flags = pick(size, 16).astype(F32)
    out = []
    for r in range(rows):
        p0 = pick(2 * r * B, B)
        p1 = pick((2 * r + 1) * B, B)
        lower = jnp.broadcast_to(flags[2 * r : 2 * r + 1, :], (B, B)).astype(BF)
        upper = jnp.broadcast_to(flags[2 * r + 1 : 2 * r + 2, :], (B, B)).astype(BF)
        out.append((p1 * lower, p0, p1 * upper))
    return out


def stack_bands(bands):
    return jnp.concatenate([jnp.concatenate(band, axis=1) for band in bands], axis=0)


def shift_at(a_cols, r, k, nfine):
    return lax.rem(a_cols[k, 0, r] - (a_cols[0, 0, 0] + r) + 3 + nfine, nfine) - 3


def flip(x):
    return jnp.transpose(x, (1, 0))


def inner_kernel(
    nfine, ncoarse, ncoarsest, ac_hbm, pc_hbm, qc_hbm, a_hbm, p_hbm, p2_hbm,
    acc_out, part_out, edge_out, wt_out, own_out, ownt_out,
    a_cols, p_cols, p2_cols, a_ref, p_ref, p2_ref, acc, prod, sems,
):
    order = (0, 3, 1, 2)
    cols_in = [
        pltpu.make_async_copy(x, y, sems.at[6 + n])
        for n, (x, y) in enumerate(((ac_hbm, a_cols), (pc_hbm, p_cols), (qc_hbm, p2_cols)))
    ]
    for copy in cols_in:
        copy.start()
    copies = [pltpu.make_async_copy(p_hbm, p_ref, sems.at[4])]
    for g in range(4):
        rows = pl.ds(4 * g * K * B, 4 * K * B)
        copies.append(pltpu.make_async_copy(a_hbm.at[rows], a_ref.at[rows], sems.at[g]))
    copies.append(pltpu.make_async_copy(p2_hbm, p2_ref, sems.at[5]))
    copies[0].start()
    for g in order:
        copies[1 + g].start()
    copies[5].start()
    for copy in cols_in:
        copy.wait()
    copies[0].wait()
    for g in order:
        copies[1 + g].wait()
        for r in range(4 * g, 4 * g + 4):
            acc[...] = jnp.zeros_like(acc)
            for k in range(K):
                v = r + shift_at(a_cols, r, k, nfine)
                inside = jnp.logical_and(v >= 0, v < ROWS)
                v = jnp.clip(v, 0, ROWS - 1)
                side = side_at(p_cols, v, ncoarse)
                slot0 = jnp.where(inside, v // 4 - g + 2, 6)
                slot1 = slot0 + side
                w0 = p_ref[pl.ds(pl.multiple_of(v * 2 * B, 2 * B), B), :]
                w1 = p_ref[pl.ds(pl.multiple_of(v * 2 * B + B, B), B), :]
                terms = dot(a_ref[blk(r * K + k), :], jnp.concatenate([w0, w1], axis=1))
                acc[slot0] += terms[:, :B]
                acc[slot1] += terms[:, B:]
            for s in range(5):
                if g in (0, 3):
                    acc_out[4 * (g // 3) + r % 4, :, s * B : (s + 1) * B] = acc[s]
                else:
                    prod[blk(r - 4), s * B : (s + 1) * B] = acc[s].astype(BF)
    for side in (0, 1):
        first = 0 if side == 0 else ROWS - 3
        for n in range(3):
            r = first + n
            for h in range(3):
                want = (h - 3 if side == 0 else ROWS + h) - r
                at = jnp.int32(0)
                found = jnp.int32(0)
                for k in range(1, K):
                    hit = (shift_at(a_cols, r, k, nfine) == want).astype(jnp.int32)
                    at = at + hit * k
                    found = found + hit
                block = a_ref[pl.ds(pl.multiple_of((r * K + at) * B, B), B), :]
                keep = jnp.where(found > 0, block, jnp.zeros_like(block))
                edge_out[blk(3 * side + n), h * B : (h + 1) * B] = keep if abs(want) <= 3 else jnp.zeros((B, B), BF)
        bands = bands_of(p_ref, p_cols, range(12 * side, 12 * side + 4), ncoarse)
        for n in range(4):
            for m in range(3):
                wt_out[blk(3 * side + m), n * B : (n + 1) * B] = flip(bands[n][m])
    copies[5].wait()
    own = bands_of(p2_ref, p2_cols, range(CROWS), ncoarsest)
    for n in range(4):
        for m in range(3):
            own_out[blk(n), m * B : (m + 1) * B] = own[n][m]
            ownt_out[blk(m), n * B : (n + 1) * B] = flip(own[n][m])
    part_out[...] = jnp.zeros_like(part_out)
    for g in (1, 2):
        bands = stack_bands(bands_of(p_ref, p_cols, range(4 * g, 4 * g + 4), ncoarse))
        terms = dot_t(bands, prod[blk(4 * (g - 1), 4), :])
        for m in range(3):
            at = slice(g * B, (g + 5) * B)
            part_out[g + m, :, at] = part_out[g + m, :, at] + terms[m * B : (m + 1) * B, :]


def outer_kernel(
    acc_in, part_in, edge, wt, own, ownt, pa, pb, qa, qb, part, fine_out, ma, mb, na, nb, prod, cp
):
    d = place()
    even = d % 2 == 0
    part[...] = part_in[...]
    for side in (0, 1):
        bands = stack_bands(
            halo_bands(pb, pa, even, 3, 6 * B) if side == 0 else halo_bands(pa, pb, even, 3, 6 * B)
        )
        terms = dot(edge[blk(3 * side, 3), :], bands)
        for n in range(4):
            r = 4 * side + n
            q = n if side == 0 else n - 1
            for s in range(5):
                value = acc_in[r, :, s * B : (s + 1) * B]
                lane = s if side == 0 else s - 2
                if 0 <= lane < 3 and 0 <= q < 3:
                    value = value + terms[q * B : (q + 1) * B, lane * B : (lane + 1) * B]
                prod[blk(r), s * B : (s + 1) * B] = value.astype(BF)
    for side in (0, 1):
        g = 3 * side
        terms = dot(wt[blk(3 * side, 3), :], prod[blk(4 * side, 4), :])
        for m in range(3):
            at = slice(g * B, (g + 5) * B)
            part[g + m, :, at] = part[g + m, :, at] + terms[m * B : (m + 1) * B, :]
    low = halo_bands(qb, qa, even, 2, 4 * B)
    high = halo_bands(qa, qb, even, 2, 4 * B)
    lines = part[...].astype(BF).reshape(6 * B, 8 * B)
    ta = dot(lines[0 : 4 * B, 0 : 2 * B], stack_bands(low))
    tb = dot(lines[:, 2 * B : 6 * B], own[...])
    tc = dot(lines[2 * B : 6 * B, 6 * B : 8 * B], stack_bands(high))
    for e in range(5):
        for i in range(6):
            pieces = []
            if e < 3 and i < 4:
                pieces.append(ta[i * B : (i + 1) * B, e * B : (e + 1) * B])
            if 1 <= e < 4:
                pieces.append(tb[i * B : (i + 1) * B, (e - 1) * B : e * B])
            if e >= 2 and i >= 2:
                pieces.append(tc[(i - 2) * B : (i - 1) * B, (e - 2) * B : (e - 1) * B])
            value = sum(pieces[1:], pieces[0]) if pieces else jnp.zeros((B, B), F32)
            cp[blk(i), e * B : (e + 1) * B] = value.astype(BF)
    gm = dot_t(stack_bands(low[1:2]), cp[blk(0), :])
    g0 = dot(ownt[...], cp[blk(1, 4), :])
    gp = dot_t(stack_bands(high[0:1]), cp[blk(5), :])

    def row(x, m):
        return x[m * B : (m + 1) * B, :]

    fine_out[...] = row(gm, 2) + row(g0, 1) + row(gp, 0)
    to_low = (row(gm, 1) + row(g0, 0)).astype(BF)
    to_high = (row(g0, 2) + row(gp, 1)).astype(BF)
    two_low = row(gm, 0).astype(BF)
    two_high = row(gp, 2).astype(BF)

    def put(dst, coarse_row, q0, fine):
        for t in range(5):
            dst[blk(t), :] = part[coarse_row, :, (q0 + t) * B : (q0 + t + 1) * B].astype(BF)
            dst[blk(5 + t), :] = fine[:, t * B : (t + 1) * B]

    def put2(dst, fine, e0):
        for t in range(4):
            dst[blk(t), :] = fine[:, (e0 + t) * B : (e0 + t + 1) * B]

    @pl.when(even)
    def _():
        put(mb, 0, 0, to_low)
        put(ma, 5, 3, to_high)

    @pl.when(jnp.logical_not(even))
    def _():
        put(ma, 0, 0, to_low)
        put(mb, 5, 3, to_high)

    even2 = (d // 2) % 2 == 0

    @pl.when(even2)
    def _():
        put2(nb, two_low, 0)
        put2(na, two_high, 1)

    @pl.when(jnp.logical_not(even2))
    def _():
        put2(na, two_low, 0)
        put2(nb, two_high, 1)


def column_block(part, j, t):
    q = t + j - 1
    if 0 <= q < 8:
        return part[j + 1, :, q * B : (q + 1) * B]
    return jnp.zeros((B, B), F32)


def store_kernel(part, coarse_hbm, rows, sems):
    copies = []
    for j in range(CROWS):
        for t in range(KC):
            rows[blk(j * KC + t), :] = column_block(part, j, t).astype(BF)
        at = blk(j * KC, KC)
        copies.append(pltpu.make_async_copy(rows.at[at], coarse_hbm.at[at], sems.at[j]))
        copies[-1].start()
    for copy in copies:
        copy.wait()


def last_kernel(coarse_in, part, fine, ma, mb, na, nb, coarse_out, coarsest_out, rows, sems):
    d = place()
    even = d % 2 == 0
    even2 = (d // 2) % 2 == 0

    def one(low, t):
        if low:
            return jnp.where(even, mb[blk(t), :], ma[blk(t), :]).astype(F32)
        return jnp.where(even, ma[blk(t), :], mb[blk(t), :]).astype(F32)

    def two(low, t):
        if low:
            return jnp.where(even2, nb[blk(t), :], na[blk(t), :]).astype(F32)
        return jnp.where(even2, na[blk(t), :], nb[blk(t), :]).astype(F32)

    for t in range(5):
        rows[blk(t), :] = (column_block(part, 0, t) + one(True, t)).astype(BF)
        rows[blk(5 + t), :] = (column_block(part, 3, t + 2) + one(False, t)).astype(BF)
    copies = [
        pltpu.make_async_copy(rows.at[blk(0, 5)], coarse_out.at[blk(0, 5)], sems.at[0]),
        pltpu.make_async_copy(rows.at[blk(5, 5)], coarse_out.at[blk(3 * KC + 2, 5)], sems.at[1]),
    ]
    for copy in copies:
        copy.start()
    for t in range(KC):
        value = jnp.zeros((B, B), F32)
        if 1 <= t < 6:
            value = value + fine[:, (t - 1) * B : t * B]
        if t < 5:
            value = value + one(True, 5 + t)
        if t >= 2:
            value = value + one(False, 5 + t - 2)
        if t < 4:
            value = value + two(True, t)
        if t >= 3:
            value = value + two(False, t - 3)
        coarsest_out[blk(t), :] = value.astype(BF)
    for copy in copies:
        copy.wait()


def call(kernel, ins, outs, args, scratch=(), cost=None, **kw):
    vmem = pl.BlockSpec(memory_space=pltpu.VMEM)
    hbm = pl.BlockSpec(memory_space=pltpu.HBM)
    kinds = {"v": vmem, "h": hbm}
    if not kw:
        args = [pltpu.with_memory_space_constraint(x, pltpu.HBM) if c == "h" else x for c, x in zip(ins, args)]
    return pl.pallas_call(
        kernel,
        in_specs=[kinds[c] for c in ins],
        out_specs=tuple(kinds[c] for c, _, _ in outs),
        out_shape=tuple(jax.ShapeDtypeStruct(shape, dtype) for _, shape, dtype in outs),
        scratch_shapes=list(scratch),
        compiler_params=pltpu.CompilerParams(vmem_limit_bytes=40 * 1024 * 1024),
        cost_estimate=cost,
        **kw,
    )(*args)


def body(a_vals, a_cols, p_vals, p_cols, p2_vals, p2_cols):
    devices = lax.axis_size(AXES)
    nfine = ROWS * devices
    ncoarse = CROWS * devices
    a_cols = jnp.transpose(a_cols, (2, 0, 1))
    p_cols = p_cols.reshape(ROWS, 2).T
    p2_cols = p2_cols.reshape(CROWS, 2).T
    a = a_vals.reshape(ROWS * K * B, B)
    p = p_vals.reshape(ROWS * 2 * B, B)
    p2 = p2_vals.reshape(CROWS * 2 * B, B)
    swap_a = [(i, i ^ 1) for i in range(devices)]
    swap_b = [(i, (i + 1) % devices if i % 2 else (i - 1) % devices) for i in range(devices)]
    skip_a = [(i, i ^ 2) for i in range(devices)]
    skip_b = [(i, (i + 2) % devices if i & 2 else (i - 2) % devices) for i in range(devices)]

    def pack(*refs):
        pack_kernel(ncoarse, devices, *refs)

    pa, pb, qa, qb = call(
        pack,
        "hhhh",
        [("v", (PM, B), BF), ("v", (PM, B), BF), ("v", (QM, B), BF), ("v", (QM, B), BF)],
        (p_cols, p2_cols, p, p2),
        [
            pltpu.SMEM((2, ROWS), jnp.int32),
            pltpu.SMEM((2, CROWS), jnp.int32),
            pltpu.SemaphoreType.DMA((6,)),
        ],
    )
    pa = lax.ppermute(pa, AXES, swap_a)
    pb = lax.ppermute(pb, AXES, swap_b)
    qa = lax.ppermute(qa, AXES, swap_a)
    qb = lax.ppermute(qb, AXES, swap_b)

    def inner(*refs):
        inner_kernel(nfine, ncoarse, devices, *refs)

    ready = call(
        inner,
        "hhhhhh",
        [
            ("v", (8, B, 5 * B), F32),
            ("v", (6, B, 8 * B), F32),
            ("v", (6 * B, 3 * B), BF),
            ("v", (6 * B, 4 * B), BF),
            ("v", (4 * B, 3 * B), BF),
            ("v", (3 * B, 4 * B), BF),
        ],
        (a_cols, p_cols, p2_cols, a, p, p2),
        [
            pltpu.SMEM((K, 1, ROWS), jnp.int32),
            pltpu.SMEM((2, ROWS), jnp.int32),
            pltpu.SMEM((2, CROWS), jnp.int32),
            pltpu.VMEM((ROWS * K * B, B), BF),
            pltpu.VMEM((ROWS * 2 * B, B), BF),
            pltpu.VMEM((CROWS * 2 * B, B), BF),
            pltpu.VMEM((8, B, B), F32),
            pltpu.VMEM((8 * B, 5 * B), BF),
            pltpu.SemaphoreType.DMA((9,)),
        ],
        pl.CostEstimate(flops=10**9, bytes_accessed=8 * 10**6, transcendentals=0),
    )
    part, fine, ma, mb, na, nb = call(
        outer_kernel,
        "vvvvvvvvvv",
        [
            ("v", (6, B, 8 * B), F32),
            ("v", (B, 5 * B), F32),
            ("v", (10 * B, B), BF),
            ("v", (10 * B, B), BF),
            ("v", (4 * B, B), BF),
            ("v", (4 * B, B), BF),
        ],
        (*ready, pa, pb, qa, qb),
        [pltpu.VMEM((8 * B, 5 * B), BF), pltpu.VMEM((6 * B, 5 * B), BF)],
        pl.CostEstimate(flops=2 * 10**9, bytes_accessed=8 * 10**6, transcendentals=0),
    )
    mb = lax.ppermute(mb, AXES, swap_b)
    nb = lax.ppermute(nb, AXES, skip_b)
    ma = lax.ppermute(ma, AXES, swap_a)
    na = lax.ppermute(na, AXES, skip_a)
    (coarse,) = call(
        store_kernel,
        "v",
        [("h", (CROWS * KC * B, B), BF)],
        (part,),
        [pltpu.VMEM((CROWS * KC * B, B), BF), pltpu.SemaphoreType.DMA((CROWS,))],
        pl.CostEstimate(flops=10**6, bytes_accessed=3 * 10**6, transcendentals=0),
    )
    coarse, coarsest = call(
        last_kernel,
        "hvvvvvv",
        [("h", (CROWS * KC * B, B), BF), ("v", (KC * B, B), BF)],
        (coarse, part, fine, ma, mb, na, nb),
        [pltpu.VMEM((10 * B, B), BF), pltpu.SemaphoreType.DMA((2,))],
        input_output_aliases={0: 0},
    )
    return coarse.reshape(1, CROWS, KC, B, B), coarsest.reshape(1, 1, KC, B, B)


def solution(mesh):
    blocks = P(None, AXES, None, None, None)
    cols = P(None, AXES, None)
    return jax.shard_map(
        body,
        mesh=mesh,
        in_specs=(blocks, cols, blocks, cols, blocks, cols),
        out_specs=(blocks, blocks),
        check_vma=False,
    )
```

```python
import jax
import jax.numpy as jnp
from jax import lax
from jax.experimental import pallas as pl
from jax.experimental.pallas import tpu as pltpu
from jax.sharding import PartitionSpec as P


B = 128
K = 5
KC = 7
ROWS = 16
CROWS = 4
BF = jnp.bfloat16
F32 = jnp.float32
PM = 10 * B + 16
AXES = ("gx", "gy")


def blk(i, n=1):
    return pl.ds(i * B, n * B)


def side_at(cols, r, ncoarse):
    return lax.rem(cols[1, r] - cols[0, r] + 1 + ncoarse, ncoarse) - 1


def place():
    return lax.axis_index(AXES)


def dot(a, b):
    return jnp.dot(a, b, preferred_element_type=F32)


def dot_t(a, b):
    return lax.dot_general(a, b, (((0,), (0,)), ((), ())), preferred_element_type=F32)


def pack_kernel(ncoarse, ncoarsest, pc_hbm, qc_hbm, p_hbm, p2_hbm, up, down, p_cols, p2_cols, sems):
    cols_in = [pltpu.make_async_copy(x, y, sems.at[4 + n]) for n, (x, y) in enumerate(((pc_hbm, p_cols), (qc_hbm, p2_cols)))]
    for copy in cols_in:
        copy.start()
    copies = []
    for n, (dst, fine, coarse) in enumerate(((up, ROWS - 3, CROWS - 2), (down, 0, 0))):
        copies.append(pltpu.make_async_copy(p_hbm.at[blk(2 * fine, 6)], dst.at[blk(0, 6)], sems.at[2 * n]))
        copies.append(pltpu.make_async_copy(p2_hbm.at[blk(2 * coarse, 4)], dst.at[blk(6, 4)], sems.at[2 * n + 1]))
    for copy in copies:
        copy.start()
    row = lax.broadcasted_iota(jnp.int32, (16, B), 0)
    for copy in cols_in:
        copy.wait()
    for dst, fine, coarse in ((up, ROWS - 3, CROWS - 2), (down, 0, 0)):
        flags = jnp.zeros((16, B), F32)
        sides = [side_at(p_cols, fine + r, ncoarse) for r in range(3)]
        sides += [side_at(p2_cols, coarse + r, ncoarsest) for r in range(2)]
        for r, side in enumerate(sides):
            flags = jnp.where(row == 2 * r, (side < 0).astype(F32), flags)
            flags = jnp.where(row == 2 * r + 1, (side > 0).astype(F32), flags)
        dst[pl.ds(10 * B, 16), :] = flags.astype(BF)
    for copy in copies:
        copy.wait()


def bands_of(p_ref, cols, rows, ncoarse):
    out = []
    for r in rows:
        side = side_at(cols, r, ncoarse)
        p0 = p_ref[blk(2 * r), :]
        p1 = p_ref[blk(2 * r + 1), :]
        zero = jnp.zeros_like(p1)
        out.append((jnp.where(side < 0, p1, zero), p0, jnp.where(side > 0, p1, zero)))
    return out


def halo_bands(message, rows):
    flags = message[pl.ds(10 * B, 16), :].astype(F32)
    out = []
    for r in rows:
        p0 = message[blk(2 * r), :]
        p1 = message[blk(2 * r + 1), :]
        lower = jnp.broadcast_to(flags[2 * r : 2 * r + 1, :], (B, B)).astype(BF)
        upper = jnp.broadcast_to(flags[2 * r + 1 : 2 * r + 2, :], (B, B)).astype(BF)
        out.append((p1 * lower, p0, p1 * upper))
    return out


def stack_bands(bands):
    return jnp.concatenate([jnp.concatenate(band, axis=1) for band in bands], axis=0)


def shift_at(a_cols, r, k, nfine):
    return lax.rem(a_cols[k, 0, r] - (a_cols[0, 0, 0] + r) + 3 + nfine, nfine) - 3


def flip(x):
    return jnp.transpose(x, (1, 0))


def inner_kernel(
    nfine, ncoarse, ncoarsest, ac_hbm, pc_hbm, qc_hbm, a_hbm, p_hbm, p2_hbm,
    acc_out, part_out, edge_out, wt_out, own_out, ownt_out,
    a_cols, p_cols, p2_cols, a_ref, p_ref, p2_ref, acc, prod, sems,
):
    order = (0, 3, 1, 2)
    cols_in = [
        pltpu.make_async_copy(x, y, sems.at[6 + n])
        for n, (x, y) in enumerate(((ac_hbm, a_cols), (pc_hbm, p_cols), (qc_hbm, p2_cols)))
    ]
    for copy in cols_in:
        copy.start()
    copies = [pltpu.make_async_copy(p_hbm, p_ref, sems.at[4])]
    for g in range(4):
        rows = pl.ds(4 * g * K * B, 4 * K * B)
        copies.append(pltpu.make_async_copy(a_hbm.at[rows], a_ref.at[rows], sems.at[g]))
    copies.append(pltpu.make_async_copy(p2_hbm, p2_ref, sems.at[5]))
    copies[0].start()
    for g in order:
        copies[1 + g].start()
    copies[5].start()
    for copy in cols_in:
        copy.wait()
    copies[0].wait()
    for g in order:
        copies[1 + g].wait()
        for r in range(4 * g, 4 * g + 4):
            acc[...] = jnp.zeros_like(acc)
            for k in range(K):
                v = r + shift_at(a_cols, r, k, nfine)
                inside = jnp.logical_and(v >= 0, v < ROWS)
                v = jnp.clip(v, 0, ROWS - 1)
                side = side_at(p_cols, v, ncoarse)
                slot0 = jnp.where(inside, v // 4 - g + 2, 6)
                slot1 = slot0 + side
                w0 = p_ref[pl.ds(pl.multiple_of(v * 2 * B, 2 * B), B), :]
                w1 = p_ref[pl.ds(pl.multiple_of(v * 2 * B + B, B), B), :]
                terms = dot(a_ref[blk(r * K + k), :], jnp.concatenate([w0, w1], axis=1))
                acc[slot0] += terms[:, :B]
                acc[slot1] += terms[:, B:]
            for s in range(5):
                if g in (0, 3):
                    acc_out[4 * (g // 3) + r % 4, :, s * B : (s + 1) * B] = acc[s]
                else:
                    prod[blk(r - 4), s * B : (s + 1) * B] = acc[s].astype(BF)
    for side in (0, 1):
        first = 0 if side == 0 else ROWS - 3
        for n in range(3):
            r = first + n
            for h in range(3):
                want = (h - 3 if side == 0 else ROWS + h) - r
                at = jnp.int32(0)
                found = jnp.int32(0)
                for k in range(1, K):
                    hit = (shift_at(a_cols, r, k, nfine) == want).astype(jnp.int32)
                    at = at + hit * k
                    found = found + hit
                block = a_ref[pl.ds(pl.multiple_of((r * K + at) * B, B), B), :]
                keep = jnp.where(found > 0, block, jnp.zeros_like(block))
                edge_out[blk(3 * side + n), h * B : (h + 1) * B] = keep if abs(want) <= 3 else jnp.zeros((B, B), BF)
        bands = bands_of(p_ref, p_cols, range(12 * side, 12 * side + 4), ncoarse)
        for n in range(4):
            for m in range(3):
                wt_out[blk(3 * side + m), n * B : (n + 1) * B] = flip(bands[n][m])
    copies[5].wait()
    own = bands_of(p2_ref, p2_cols, range(CROWS), ncoarsest)
    for n in range(4):
        for m in range(3):
            own_out[blk(n), m * B : (m + 1) * B] = own[n][m]
            ownt_out[blk(m), n * B : (n + 1) * B] = flip(own[n][m])
    part_out[...] = jnp.zeros_like(part_out)
    for g in (1, 2):
        bands = stack_bands(bands_of(p_ref, p_cols, range(4 * g, 4 * g + 4), ncoarse))
        terms = dot_t(bands, prod[blk(4 * (g - 1), 4), :])
        for m in range(3):
            at = slice(g * B, (g + 5) * B)
            part_out[g + m, :, at] = part_out[g + m, :, at] + terms[m * B : (m + 1) * B, :]


def outer_kernel(
    acc_in, part_in, edge, wt, own, ownt, from_low, from_high, part, fine_out, ma, mb, na, nb, prod, cp
):
    d = place()
    even = d % 2 == 0
    part[...] = part_in[...]
    for side in (0, 1):
        bands = stack_bands(halo_bands(from_low if side == 0 else from_high, range(3)))
        terms = dot(edge[blk(3 * side, 3), :], bands)
        for n in range(4):
            r = 4 * side + n
            q = n if side == 0 else n - 1
            for s in range(5):
                value = acc_in[r, :, s * B : (s + 1) * B]
                lane = s if side == 0 else s - 2
                if 0 <= lane < 3 and 0 <= q < 3:
                    value = value + terms[q * B : (q + 1) * B, lane * B : (lane + 1) * B]
                prod[blk(r), s * B : (s + 1) * B] = value.astype(BF)
    for side in (0, 1):
        g = 3 * side
        terms = dot(wt[blk(3 * side, 3), :], prod[blk(4 * side, 4), :])
        for m in range(3):
            at = slice(g * B, (g + 5) * B)
            part[g + m, :, at] = part[g + m, :, at] + terms[m * B : (m + 1) * B, :]
    low = halo_bands(from_low, (3, 4))
    high = halo_bands(from_high, (3, 4))
    lines = part[...].astype(BF).reshape(6 * B, 8 * B)
    ta = dot(lines[0 : 4 * B, 0 : 2 * B], stack_bands(low))
    tb = dot(lines[:, 2 * B : 6 * B], own[...])
    tc = dot(lines[2 * B : 6 * B, 6 * B : 8 * B], stack_bands(high))
    for e in range(5):
        for i in range(6):
            pieces = []
            if e < 3 and i < 4:
                pieces.append(ta[i * B : (i + 1) * B, e * B : (e + 1) * B])
            if 1 <= e < 4:
                pieces.append(tb[i * B : (i + 1) * B, (e - 1) * B : e * B])
            if e >= 2 and i >= 2:
                pieces.append(tc[(i - 2) * B : (i - 1) * B, (e - 2) * B : (e - 1) * B])
            value = sum(pieces[1:], pieces[0]) if pieces else jnp.zeros((B, B), F32)
            cp[blk(i), e * B : (e + 1) * B] = value.astype(BF)
    gm = dot_t(stack_bands(low[1:2]), cp[blk(0), :])
    g0 = dot(ownt[...], cp[blk(1, 4), :])
    gp = dot_t(stack_bands(high[0:1]), cp[blk(5), :])

    def row(x, m):
        return x[m * B : (m + 1) * B, :]

    fine_out[...] = row(gm, 2) + row(g0, 1) + row(gp, 0)
    to_low = (row(gm, 1) + row(g0, 0)).astype(BF)
    to_high = (row(g0, 2) + row(gp, 1)).astype(BF)
    two_low = row(gm, 0).astype(BF)
    two_high = row(gp, 2).astype(BF)

    def put(dst, coarse_row, q0, fine):
        for t in range(5):
            dst[blk(t), :] = part[coarse_row, :, (q0 + t) * B : (q0 + t + 1) * B].astype(BF)
            dst[blk(5 + t), :] = fine[:, t * B : (t + 1) * B]

    def put2(dst, fine, e0):
        for t in range(4):
            dst[blk(t), :] = fine[:, (e0 + t) * B : (e0 + t + 1) * B]

    @pl.when(even)
    def _():
        put(mb, 0, 0, to_low)
        put(ma, 5, 3, to_high)

    @pl.when(jnp.logical_not(even))
    def _():
        put(ma, 0, 0, to_low)
        put(mb, 5, 3, to_high)

    even2 = (d // 2) % 2 == 0

    @pl.when(even2)
    def _():
        put2(nb, two_low, 0)
        put2(na, two_high, 1)

    @pl.when(jnp.logical_not(even2))
    def _():
        put2(na, two_low, 0)
        put2(nb, two_high, 1)


def column_block(part, j, t):
    q = t + j - 1
    if 0 <= q < 8:
        return part[j + 1, :, q * B : (q + 1) * B]
    return jnp.zeros((B, B), F32)


def store_kernel(part, coarse_hbm, rows, sems):
    copies = []
    for j in range(CROWS):
        for t in range(KC):
            rows[blk(j * KC + t), :] = column_block(part, j, t).astype(BF)
        at = blk(j * KC, KC)
        copies.append(pltpu.make_async_copy(rows.at[at], coarse_hbm.at[at], sems.at[j]))
        copies[-1].start()
    for copy in copies:
        copy.wait()


def last_kernel(coarse_in, part, fine, ma, mb, na, nb, coarse_out, coarsest_out, rows, sems):
    d = place()
    even = d % 2 == 0
    even2 = (d // 2) % 2 == 0

    def one(low, t):
        if low:
            return jnp.where(even, mb[blk(t), :], ma[blk(t), :]).astype(F32)
        return jnp.where(even, ma[blk(t), :], mb[blk(t), :]).astype(F32)

    def two(low, t):
        if low:
            return jnp.where(even2, nb[blk(t), :], na[blk(t), :]).astype(F32)
        return jnp.where(even2, na[blk(t), :], nb[blk(t), :]).astype(F32)

    for t in range(5):
        rows[blk(t), :] = (column_block(part, 0, t) + one(True, t)).astype(BF)
        rows[blk(5 + t), :] = (column_block(part, 3, t + 2) + one(False, t)).astype(BF)
    copies = [
        pltpu.make_async_copy(rows.at[blk(0, 5)], coarse_out.at[blk(0, 5)], sems.at[0]),
        pltpu.make_async_copy(rows.at[blk(5, 5)], coarse_out.at[blk(3 * KC + 2, 5)], sems.at[1]),
    ]
    for copy in copies:
        copy.start()
    for t in range(KC):
        value = jnp.zeros((B, B), F32)
        if 1 <= t < 6:
            value = value + fine[:, (t - 1) * B : t * B]
        if t < 5:
            value = value + one(True, 5 + t)
        if t >= 2:
            value = value + one(False, 5 + t - 2)
        if t < 4:
            value = value + two(True, t)
        if t >= 3:
            value = value + two(False, t - 3)
        coarsest_out[blk(t), :] = value.astype(BF)
    for copy in copies:
        copy.wait()


def call(kernel, ins, outs, args, scratch=(), cost=None, **kw):
    vmem = pl.BlockSpec(memory_space=pltpu.VMEM)
    hbm = pl.BlockSpec(memory_space=pltpu.HBM)
    kinds = {"v": vmem, "h": hbm}
    if not kw:
        args = [pltpu.with_memory_space_constraint(x, pltpu.HBM) if c == "h" else x for c, x in zip(ins, args)]
    return pl.pallas_call(
        kernel,
        in_specs=[kinds[c] for c in ins],
        out_specs=tuple(kinds[c] for c, _, _ in outs),
        out_shape=tuple(jax.ShapeDtypeStruct(shape, dtype) for _, shape, dtype in outs),
        scratch_shapes=list(scratch),
        compiler_params=pltpu.CompilerParams(vmem_limit_bytes=40 * 1024 * 1024),
        cost_estimate=cost,
        **kw,
    )(*args)


def body(a_vals, a_cols, p_vals, p_cols, p2_vals, p2_cols):
    devices = lax.axis_size(AXES)
    nfine = ROWS * devices
    ncoarse = CROWS * devices
    a_cols = jnp.transpose(a_cols, (2, 0, 1))
    p_cols = p_cols.reshape(ROWS, 2).T
    p2_cols = p2_cols.reshape(CROWS, 2).T
    a = a_vals.reshape(ROWS * K * B, B)
    p = p_vals.reshape(ROWS * 2 * B, B)
    p2 = p2_vals.reshape(CROWS * 2 * B, B)
    swap_a = [(i, i ^ 1) for i in range(devices)]
    swap_b = [(i, (i + 1) % devices if i % 2 else (i - 1) % devices) for i in range(devices)]
    skip_a = [(i, i ^ 2) for i in range(devices)]
    skip_b = [(i, (i + 2) % devices if i & 2 else (i - 2) % devices) for i in range(devices)]

    def pack(*refs):
        pack_kernel(ncoarse, devices, *refs)

    up, down = call(
        pack,
        "hhhh",
        [("v", (PM, B), BF), ("v", (PM, B), BF)],
        (p_cols, p2_cols, p, p2),
        [
            pltpu.SMEM((2, ROWS), jnp.int32),
            pltpu.SMEM((2, CROWS), jnp.int32),
            pltpu.SemaphoreType.DMA((6,)),
        ],
    )
    from_low = lax.ppermute(up, AXES, [(i, (i + 1) % devices) for i in range(devices)])
    from_high = lax.ppermute(down, AXES, [((i + 1) % devices, i) for i in range(devices)])

    def inner(*refs):
        inner_kernel(nfine, ncoarse, devices, *refs)

    ready = call(
        inner,
        "hhhhhh",
        [
            ("v", (8, B, 5 * B), F32),
            ("v", (6, B, 8 * B), F32),
            ("v", (6 * B, 3 * B), BF),
            ("v", (6 * B, 4 * B), BF),
            ("v", (4 * B, 3 * B), BF),
            ("v", (3 * B, 4 * B), BF),
        ],
        (a_cols, p_cols, p2_cols, a, p, p2),
        [
            pltpu.SMEM((K, 1, ROWS), jnp.int32),
            pltpu.SMEM((2, ROWS), jnp.int32),
            pltpu.SMEM((2, CROWS), jnp.int32),
            pltpu.VMEM((ROWS * K * B, B), BF),
            pltpu.VMEM((ROWS * 2 * B, B), BF),
            pltpu.VMEM((CROWS * 2 * B, B), BF),
            pltpu.VMEM((8, B, B), F32),
            pltpu.VMEM((8 * B, 5 * B), BF),
            pltpu.SemaphoreType.DMA((9,)),
        ],
        pl.CostEstimate(flops=10**9, bytes_accessed=8 * 10**6, transcendentals=0),
    )
    part, fine, ma, mb, na, nb = call(
        outer_kernel,
        "vvvvvvvv",
        [
            ("v", (6, B, 8 * B), F32),
            ("v", (B, 5 * B), F32),
            ("v", (10 * B, B), BF),
            ("v", (10 * B, B), BF),
            ("v", (4 * B, B), BF),
            ("v", (4 * B, B), BF),
        ],
        (*ready, from_low, from_high),
        [pltpu.VMEM((8 * B, 5 * B), BF), pltpu.VMEM((6 * B, 5 * B), BF)],
        pl.CostEstimate(flops=2 * 10**9, bytes_accessed=8 * 10**6, transcendentals=0),
    )
    mb = lax.ppermute(mb, AXES, swap_b)
    nb = lax.ppermute(nb, AXES, skip_b)
    ma = lax.ppermute(ma, AXES, swap_a)
    na = lax.ppermute(na, AXES, skip_a)
    (coarse,) = call(
        store_kernel,
        "v",
        [("h", (CROWS * KC * B, B), BF)],
        (part,),
        [pltpu.VMEM((CROWS * KC * B, B), BF), pltpu.SemaphoreType.DMA((CROWS,))],
        pl.CostEstimate(flops=10**6, bytes_accessed=3 * 10**6, transcendentals=0),
    )
    coarse, coarsest = call(
        last_kernel,
        "hvvvvvv",
        [("h", (CROWS * KC * B, B), BF), ("v", (KC * B, B), BF)],
        (coarse, part, fine, ma, mb, na, nb),
        [pltpu.VMEM((10 * B, B), BF), pltpu.SemaphoreType.DMA((2,))],
        input_output_aliases={0: 0},
    )
    return coarse.reshape(1, CROWS, KC, B, B), coarsest.reshape(1, 1, KC, B, B)


def solution(mesh):
    blocks = P(None, AXES, None, None, None)
    cols = P(None, AXES, None)

    return jax.shard_map(
        body,
        mesh=mesh,
        in_specs=(blocks, cols, blocks, cols, blocks, cols),
        out_specs=(blocks, blocks),
        check_vma=False,
    )
```

```python
import jax
import jax.numpy as jnp
from jax import lax
from jax.experimental import pallas as pl
from jax.experimental.pallas import tpu as pltpu
from jax.sharding import PartitionSpec as P


B = 128
K = 5
KC = 7
ROWS = 16
CROWS = 4
BF = jnp.bfloat16
F32 = jnp.float32
PM = 6 * B + 16
QM = 4 * B + 16
NACC = 8
AXES = ("gx", "gy")


def blk(i, n=1):
    return pl.ds(i * B, n * B)


def side_at(cols, r, ncoarse):
    step = cols[1, r] - cols[0, r]
    return jnp.where(jnp.logical_or(step == 1, step == 1 - ncoarse), 1, -1)


def place():
    return lax.axis_index(AXES)


def dot(a, b):
    return jnp.dot(a, b, preferred_element_type=F32)


def dot_t(a, b):
    return lax.dot_general(a, b, (((0,), (0,)), ((), ())), preferred_element_type=F32)


def pack_kernel(ncoarse, ncoarsest, pc_hbm, qc_hbm, p_hbm, p2_hbm, pu, qu, pd, qd, p_cols, p2_cols, sems):
    cols_in = [pltpu.make_async_copy(x, y, sems.at[4 + n]) for n, (x, y) in enumerate(((pc_hbm, p_cols), (qc_hbm, p2_cols)))]
    for copy in cols_in:
        copy.start()
    jobs = (
        (pu, p_hbm, p_cols, ncoarse, ROWS - 3, 3),
        (qu, p2_hbm, p2_cols, ncoarsest, CROWS - 2, 2),
        (pd, p_hbm, p_cols, ncoarse, 0, 3),
        (qd, p2_hbm, p2_cols, ncoarsest, 0, 2),
    )
    copies = [
        pltpu.make_async_copy(src.at[blk(2 * first, 2 * rows)], dst.at[blk(0, 2 * rows)], sems.at[n])
        for n, (dst, src, cols, ncols, first, rows) in enumerate(jobs)
    ]
    for copy in copies:
        copy.start()
    row = lax.broadcasted_iota(jnp.int32, (16, B), 0)
    for copy in cols_in:
        copy.wait()
    for dst, src, cols, ncols, first, rows in jobs:
        flags = jnp.zeros((16, B), F32)
        for r in range(rows):
            side = side_at(cols, first + r, ncols)
            flags = jnp.where(row == 2 * r, (side < 0).astype(F32), flags)
            flags = jnp.where(row == 2 * r + 1, (side > 0).astype(F32), flags)
        dst[pl.ds(2 * rows * B, 16), :] = flags.astype(BF)
    for copy in copies:
        copy.wait()


def bands_of(p_ref, cols, rows, ncoarse):
    out = []
    for r in rows:
        side = side_at(cols, r, ncoarse)
        p0 = p_ref[blk(2 * r), :]
        p1 = p_ref[blk(2 * r + 1), :]
        zero = jnp.zeros_like(p1)
        out.append((jnp.where(side < 0, p1, zero), p0, jnp.where(side > 0, p1, zero)))
    return out


def halo_bands(message, rows):
    flags = message[pl.ds(2 * rows * B, 16), :].astype(F32)
    out = []
    for r in range(rows):
        p0 = message[blk(2 * r), :]
        p1 = message[blk(2 * r + 1), :]
        lower = jnp.broadcast_to(flags[2 * r : 2 * r + 1, :], (B, B)).astype(BF)
        upper = jnp.broadcast_to(flags[2 * r + 1 : 2 * r + 2, :], (B, B)).astype(BF)
        out.append((p1 * lower, p0, p1 * upper))
    return out


def stack_bands(bands):
    return jnp.concatenate([jnp.concatenate(band, axis=1) for band in bands], axis=0)


def shift_at(a_cols, r, k, nfine):
    step = a_cols[k, 0, r] - a_cols[0, 0, r]
    return jnp.where(step > 3, step - nfine, jnp.where(step < -3, step + nfine, step))


def flip(x):
    return jnp.transpose(x, (1, 0))


def is_early():
    return lax.axis_index("gy") % 4 == 0


def group_products(g, a_cols, p_cols, a_ref, p_ref, accs, nfine, ncoarse, store):
    for r in range(4 * g, 4 * g + 4):
        acc = accs[r % len(accs)]
        for s in range(5):
            acc[s] = jnp.zeros((B, B), F32)
        for k in range(K):
            if k == 0:
                v, side, slot0 = r, side_at(p_cols, r, ncoarse), 2
                w0, w1 = p_ref[blk(2 * r), :], p_ref[blk(2 * r + 1), :]
            else:
                v = r + shift_at(a_cols, r, k, nfine)
                inside = jnp.logical_and(v >= 0, v < ROWS)
                v = jnp.clip(v, 0, ROWS - 1)
                side = side_at(p_cols, v, ncoarse)
                slot0 = jnp.where(inside, lax.shift_right_logical(v, 2) - g + 2, 6)
                w0 = p_ref[pl.ds(pl.multiple_of(v * 2 * B, 2 * B), B), :]
                w1 = p_ref[pl.ds(pl.multiple_of(v * 2 * B + B, B), B), :]
            terms = dot(a_ref[blk(r * K + k), :], jnp.concatenate([w0, w1], axis=1))
            acc[slot0] += terms[:, :B]
            acc[slot0 + side] += terms[:, B:]
        for s in range(5):
            store(r, s, acc[s])


def group_rows(g):
    return pl.ds(4 * g * K * B, 4 * K * B)


def start_all(pairs, sems):
    copies = [pltpu.make_async_copy(src, dst, sems.at[n]) for n, (src, dst) in enumerate(pairs)]
    for copy in copies:
        copy.start()
    return copies


def early_kernel(nfine, ncoarse, ac_hbm, pc_hbm, a_hbm, p_hbm, prod, a_cols, p_cols, a_ref, p_ref, sems, *accs):
    @pl.when(is_early())
    def _():
        pairs = [(ac_hbm, a_cols), (pc_hbm, p_cols), (p_hbm, p_ref)]
        pairs += [(a_hbm.at[group_rows(g)], a_ref.at[group_rows(g)]) for g in (0, 3)]
        for copy in start_all(pairs, sems):
            copy.wait()

        def store(r, s, value):
            prod[blk(4 * (r // 12) + r % 4), s * B : (s + 1) * B] = value.astype(BF)

        for g in (0, 3):
            group_products(g, a_cols, p_cols, a_ref, p_ref, accs, nfine, ncoarse, store)


def inner_kernel(
    nfine, ncoarse, ncoarsest, prod_in, ac_hbm, pc_hbm, qc_hbm, a_hbm, p_hbm, p2_hbm,
    prod, part_out, edge_out, wt_out, own_out, ownt_out,
    a_cols, p_cols, p2_cols, a_ref, p_ref, p2_ref, middle, sems, *accs,
):
    pairs = [(ac_hbm, a_cols), (pc_hbm, p_cols), (qc_hbm, p2_cols), (p_hbm, p_ref)]
    pairs += [(a_hbm.at[group_rows(g)], a_ref.at[group_rows(g)]) for g in (0, 3, 1, 2)]
    pairs += [(p2_hbm, p2_ref)]
    copies = start_all(pairs, sems)
    for copy in copies[:6]:
        copy.wait()

    @pl.when(jnp.logical_not(is_early()))
    def _():
        def store(r, s, value):
            prod[blk(4 * (r // 12) + r % 4), s * B : (s + 1) * B] = value.astype(BF)

        for g in (0, 3):
            group_products(g, a_cols, p_cols, a_ref, p_ref, accs, nfine, ncoarse, store)

    for copy in copies[6:]:
        copy.wait()

    def store_middle(r, s, value):
        middle[blk(r - 4), s * B : (s + 1) * B] = value.astype(BF)

    for g in (1, 2):
        group_products(g, a_cols, p_cols, a_ref, p_ref, accs, nfine, ncoarse, store_middle)
    for side in (0, 1):
        first = 0 if side == 0 else ROWS - 3
        for n in range(3):
            r = first + n
            for h in range(3):
                want = (h - 3 if side == 0 else ROWS + h) - r
                at = jnp.int32(0)
                found = jnp.int32(0)
                for k in range(1, K):
                    hit = (shift_at(a_cols, r, k, nfine) == want).astype(jnp.int32)
                    at = at + hit * k
                    found = found + hit
                block = a_ref[pl.ds(pl.multiple_of((r * K + at) * B, B), B), :]
                keep = jnp.where(found > 0, block, jnp.zeros_like(block))
                edge_out[blk(3 * side + n), h * B : (h + 1) * B] = keep if abs(want) <= 3 else jnp.zeros((B, B), BF)
        bands = bands_of(p_ref, p_cols, range(first, first + 3), ncoarse)
        for n in range(3):
            for m in range(3):
                wt_out[blk(3 * side + m), n * B : (n + 1) * B] = flip(bands[n][m])
    own = bands_of(p2_ref, p2_cols, range(CROWS), ncoarsest)
    for n in range(4):
        for m in range(3):
            own_out[blk(n), m * B : (m + 1) * B] = own[n][m]
            ownt_out[blk(m), n * B : (n + 1) * B] = flip(own[n][m])
    part_out[...] = jnp.zeros_like(part_out)
    for g in (1, 2, 0, 3):
        bands = stack_bands(bands_of(p_ref, p_cols, range(4 * g, 4 * g + 4), ncoarse))
        rows = middle[blk(4 * (g - 1), 4), :] if g in (1, 2) else prod[blk(4 * (g // 3), 4), :]
        terms = dot_t(bands, rows)
        for m in range(3):
            at = slice(g * B, (g + 5) * B)
            part_out[g + m, :, at] = part_out[g + m, :, at] + terms[m * B : (m + 1) * B, :]


def middle_kernel(part_in, edge, wt, p_low, p_high, part):
    for side in (0, 1):
        halo = stack_bands(halo_bands(p_high if side else p_low, 3))
        extra = dot(edge[blk(3 * side, 3), :], halo).astype(BF)
        terms = dot(wt[blk(3 * side, 3), :], extra)
        for m in range(3):
            j = 3 * side + m
            at = slice(5 * side * B, (5 * side + 3) * B)
            part[j, :, at] = part_in[j, :, at] + terms[m * B : (m + 1) * B, :]


def outer_kernel(part, own, ownt, q_low, q_high, fine_out, ma, mb, na, nb, cp):
    d = place()
    even = d % 2 == 0
    low = halo_bands(q_low, 2)
    high = halo_bands(q_high, 2)
    lines = part[...].astype(BF).reshape(6 * B, 8 * B)
    ta = dot(lines[0 : 4 * B, 0 : 2 * B], stack_bands(low))
    tb = dot(lines[:, 2 * B : 6 * B], own[...])
    tc = dot(lines[2 * B : 6 * B, 6 * B : 8 * B], stack_bands(high))
    for e in range(5):
        for i in range(6):
            pieces = []
            if e < 3 and i < 4:
                pieces.append(ta[i * B : (i + 1) * B, e * B : (e + 1) * B])
            if 1 <= e < 4:
                pieces.append(tb[i * B : (i + 1) * B, (e - 1) * B : e * B])
            if e >= 2 and i >= 2:
                pieces.append(tc[(i - 2) * B : (i - 1) * B, (e - 2) * B : (e - 1) * B])
            value = sum(pieces[1:], pieces[0]) if pieces else jnp.zeros((B, B), F32)
            cp[blk(i), e * B : (e + 1) * B] = value.astype(BF)
    gm = dot_t(stack_bands(low[1:2]), cp[blk(0), 0 : 4 * B])
    g0 = dot(ownt[...], cp[blk(1, 4), :])
    gp = dot_t(stack_bands(high[0:1]), cp[blk(5), B : 5 * B])

    def low_at(m, e):
        return gm[m * B : (m + 1) * B, e * B : (e + 1) * B] if e < 4 else 0.0

    def own_at(m, e):
        return g0[m * B : (m + 1) * B, e * B : (e + 1) * B]

    def high_at(m, e):
        return gp[m * B : (m + 1) * B, (e - 1) * B : e * B] if e > 0 else 0.0

    for e in range(5):
        fine_out[:, e * B : (e + 1) * B] = low_at(2, e) + own_at(1, e) + high_at(0, e)
    to_low = [(low_at(1, e) + own_at(0, e)).astype(BF) for e in range(5)]
    to_high = [(own_at(2, e) + high_at(1, e)).astype(BF) for e in range(5)]
    two_low = [low_at(0, e).astype(BF) for e in range(4)]
    two_high = [high_at(2, e).astype(BF) for e in range(1, 5)]

    def put(dst, coarse_row, q0, fine):
        for t in range(5):
            dst[blk(t), :] = part[coarse_row, :, (q0 + t) * B : (q0 + t + 1) * B].astype(BF)
            dst[blk(5 + t), :] = fine[t]

    def put2(dst, fine):
        for t in range(4):
            dst[blk(t), :] = fine[t]

    @pl.when(even)
    def _():
        put(mb, 0, 0, to_low)
        put(ma, 5, 3, to_high)

    @pl.when(jnp.logical_not(even))
    def _():
        put(ma, 0, 0, to_low)
        put(mb, 5, 3, to_high)

    even2 = (d // 2) % 2 == 0

    @pl.when(even2)
    def _():
        put2(nb, two_low)
        put2(na, two_high)

    @pl.when(jnp.logical_not(even2))
    def _():
        put2(na, two_low)
        put2(nb, two_high)


def column_block(part, j, t):
    q = t + j - 1
    if 0 <= q < 8:
        return part[j + 1, :, q * B : (q + 1) * B]
    return jnp.zeros((B, B), F32)


def store_kernel(part, coarse_hbm, rows, sems):
    copies = []
    for j in range(CROWS):
        for t in range(KC):
            rows[blk(j * KC + t), :] = column_block(part, j, t).astype(BF)
        at = blk(j * KC, KC)
        copies.append(pltpu.make_async_copy(rows.at[at], coarse_hbm.at[at], sems.at[j]))
        copies[-1].start()
    for copy in copies:
        copy.wait()


def last_kernel(coarse_in, part, fine, ma, mb, na, nb, coarse_out, coarsest_out, rows, sems):
    d = place()
    even = d % 2 == 0
    even2 = (d // 2) % 2 == 0

    def one(low, t):
        if low:
            return jnp.where(even, mb[blk(t), :], ma[blk(t), :]).astype(F32)
        return jnp.where(even, ma[blk(t), :], mb[blk(t), :]).astype(F32)

    def two(low, t):
        if low:
            return jnp.where(even2, nb[blk(t), :], na[blk(t), :]).astype(F32)
        return jnp.where(even2, na[blk(t), :], nb[blk(t), :]).astype(F32)

    for t in range(KC):
        value = jnp.zeros((B, B), F32)
        if 1 <= t < 6:
            value = value + fine[:, (t - 1) * B : t * B]
        if t < 5:
            value = value + one(True, 5 + t)
        if t >= 2:
            value = value + one(False, 5 + t - 2)
        if t < 4:
            value = value + two(True, t)
        if t >= 3:
            value = value + two(False, t - 3)
        rows[blk(10 + t), :] = value.astype(BF)
    copies = [pltpu.make_async_copy(rows.at[blk(10, KC)], coarsest_out, sems.at[2])]
    copies[0].start()
    for n, j in enumerate((0, 3)):
        for t in range(5):
            rows[blk(5 * n + t), :] = (column_block(part, j, t + 2 * n) + one(n == 0, t)).astype(BF)
        at = blk(j * KC + 2 * n, 5)
        copies.append(pltpu.make_async_copy(rows.at[blk(5 * n, 5)], coarse_out.at[at], sems.at[n]))
        copies[-1].start()
    for copy in copies:
        copy.wait()


def call(kernel, ins, outs, args, scratch=(), cost=None, **kw):
    vmem = pl.BlockSpec(memory_space=pltpu.VMEM)
    hbm = pl.BlockSpec(memory_space=pltpu.HBM)
    kinds = {"v": vmem, "h": hbm}
    aliased = kw.get("input_output_aliases", {})
    args = [
        pltpu.with_memory_space_constraint(x, pltpu.HBM) if c == "h" and n not in aliased else x
        for n, (c, x) in enumerate(zip(ins, args))
    ]
    return pl.pallas_call(
        kernel,
        in_specs=[kinds[c] for c in ins],
        out_specs=tuple(kinds[c] for c, _, _ in outs),
        out_shape=tuple(jax.ShapeDtypeStruct(shape, dtype) for _, shape, dtype in outs),
        scratch_shapes=list(scratch),
        compiler_params=pltpu.CompilerParams(vmem_limit_bytes=40 * 1024 * 1024),
        cost_estimate=cost,
        **kw,
    )(*args)


def body(a_vals, a_cols, p_vals, p_cols, p2_vals, p2_cols):
    devices = lax.axis_size(AXES)
    nfine = ROWS * devices
    ncoarse = CROWS * devices
    a_cols = jnp.transpose(a_cols, (2, 0, 1))
    p_cols = p_cols.reshape(ROWS, 2).T
    p2_cols = p2_cols.reshape(CROWS, 2).T
    a = a_vals.reshape(ROWS * K * B, B)
    p = p_vals.reshape(ROWS * 2 * B, B)
    p2 = p2_vals.reshape(CROWS * 2 * B, B)
    swap_a = [(i, i ^ 1) for i in range(devices)]
    swap_b = [(i, (i + 1) % devices if i % 2 else (i - 1) % devices) for i in range(devices)]
    skip_a = [(i, i ^ 2) for i in range(devices)]
    skip_b = [(i, (i + 2) % devices if i & 2 else (i - 2) % devices) for i in range(devices)]

    def pack(*refs):
        pack_kernel(ncoarse, devices, *refs)

    pu, qu, pd, qd = call(
        pack,
        "hhhh",
        [("v", (PM, B), BF), ("v", (QM, B), BF), ("v", (PM, B), BF), ("v", (QM, B), BF)],
        (p_cols, p2_cols, p, p2),
        [
            pltpu.SMEM((2, ROWS), jnp.int32),
            pltpu.SMEM((2, CROWS), jnp.int32),
            pltpu.SemaphoreType.DMA((6,)),
        ],
    )
    up = [(i, (i + 1) % devices) for i in range(devices)]
    down = [((i + 1) % devices, i) for i in range(devices)]
    p_low = lax.ppermute(pu, AXES, up)
    q_low = lax.ppermute(qu, AXES, up)

    def early(*refs):
        early_kernel(nfine, ncoarse, *refs)

    (prod,) = call(
        early,
        "hhhh",
        [("v", (8 * B, 5 * B), BF)],
        (a_cols, p_cols, a, p),
        [
            pltpu.SMEM((K, 1, ROWS), jnp.int32),
            pltpu.SMEM((2, ROWS), jnp.int32),
            pltpu.VMEM((ROWS * K * B, B), BF),
            pltpu.VMEM((ROWS * 2 * B, B), BF),
            pltpu.SemaphoreType.DMA((5,)),
            *[pltpu.VMEM((8, B, B), F32) for _ in range(NACC)],
        ],
        pl.CostEstimate(flops=10**6, bytes_accessed=10**6, transcendentals=0),
    )
    p_high = lax.ppermute(pd, AXES, down)
    q_high = lax.ppermute(qd, AXES, down)

    def inner(*refs):
        inner_kernel(nfine, ncoarse, devices, *refs)

    prod, part, edge, wt, own, ownt = call(
        inner,
        "vhhhhhh",
        [
            ("v", (8 * B, 5 * B), BF),
            ("v", (6, B, 8 * B), F32),
            ("v", (6 * B, 3 * B), BF),
            ("v", (6 * B, 3 * B), BF),
            ("v", (4 * B, 3 * B), BF),
            ("v", (3 * B, 4 * B), BF),
        ],
        (prod, a_cols, p_cols, p2_cols, a, p, p2),
        [
            pltpu.SMEM((K, 1, ROWS), jnp.int32),
            pltpu.SMEM((2, ROWS), jnp.int32),
            pltpu.SMEM((2, CROWS), jnp.int32),
            pltpu.VMEM((ROWS * K * B, B), BF),
            pltpu.VMEM((ROWS * 2 * B, B), BF),
            pltpu.VMEM((CROWS * 2 * B, B), BF),
            pltpu.VMEM((8 * B, 5 * B), BF),
            pltpu.SemaphoreType.DMA((9,)),
            *[pltpu.VMEM((8, B, B), F32) for _ in range(NACC)],
        ],
        pl.CostEstimate(flops=10**9, bytes_accessed=8 * 10**6, transcendentals=0),
        input_output_aliases={0: 0},
    )
    (part,) = call(
        middle_kernel,
        "vvvvv",
        [("v", (6, B, 8 * B), F32)],
        (part, edge, wt, p_low, p_high),
        cost=pl.CostEstimate(flops=10**9, bytes_accessed=4 * 10**6, transcendentals=0),
        input_output_aliases={0: 0},
    )
    fine, ma, mb, na, nb = call(
        outer_kernel,
        "vvvvv",
        [
            ("v", (B, 5 * B), F32),
            ("v", (10 * B, B), BF),
            ("v", (10 * B, B), BF),
            ("v", (4 * B, B), BF),
            ("v", (4 * B, B), BF),
        ],
        (part, own, ownt, q_low, q_high),
        [pltpu.VMEM((6 * B, 5 * B), BF)],
        pl.CostEstimate(flops=10**9, bytes_accessed=4 * 10**6, transcendentals=0),
    )
    mb = lax.ppermute(mb, AXES, swap_b)
    nb = lax.ppermute(nb, AXES, skip_b)
    ma = lax.ppermute(ma, AXES, swap_a)
    na = lax.ppermute(na, AXES, skip_a)
    (coarse,) = call(
        store_kernel,
        "v",
        [("h", (CROWS * KC * B, B), BF)],
        (part,),
        [pltpu.VMEM((CROWS * KC * B, B), BF), pltpu.SemaphoreType.DMA((CROWS,))],
        pl.CostEstimate(flops=10**6, bytes_accessed=3 * 10**6, transcendentals=0),
    )
    coarse, coarsest = call(
        last_kernel,
        "hvvvvvv",
        [("h", (CROWS * KC * B, B), BF), ("h", (KC * B, B), BF)],
        (coarse, part, fine, ma, mb, na, nb),
        [pltpu.VMEM(((10 + KC) * B, B), BF), pltpu.SemaphoreType.DMA((3,))],
        input_output_aliases={0: 0},
    )
    return coarse.reshape(1, CROWS, KC, B, B), coarsest.reshape(1, 1, KC, B, B)


def solution(mesh):
    blocks = P(None, AXES, None, None, None)
    cols = P(None, AXES, None)

    return jax.shard_map(
        body,
        mesh=mesh,
        in_specs=(blocks, cols, blocks, cols, blocks, cols),
        out_specs=(blocks, blocks),
        check_vma=False,
    )
```

```python
import jax
import jax.numpy as jnp
from jax import lax
from jax.experimental import pallas as pl
from jax.experimental.pallas import tpu as pltpu
from jax.sharding import PartitionSpec as P


B = 128
K = 5
KC = 7
ROWS = 16
CROWS = 4
BF = jnp.bfloat16
F32 = jnp.float32
PM = 6 * B + 16
QM = 4 * B + 16
NACC = 8
AXES = ("gx", "gy")


def blk(i, n=1):
    return pl.ds(i * B, n * B)


def side_at(cols, r, ncoarse):
    step = cols[1, r] - cols[0, r]
    return jnp.where(jnp.logical_or(step == 1, step == 1 - ncoarse), 1, -1)


def dot(a, b):
    return jnp.dot(a, b, preferred_element_type=F32)


def dot_t(a, b):
    return lax.dot_general(a, b, (((0,), (0,)), ((), ())), preferred_element_type=F32)


def pack_kernel(ncoarse, ncoarsest, pc_hbm, qc_hbm, p_hbm, p2_hbm, pu, qu, pd, qd, p_cols, p2_cols, sems):
    cols_in = [pltpu.make_async_copy(x, y, sems.at[4 + n]) for n, (x, y) in enumerate(((pc_hbm, p_cols), (qc_hbm, p2_cols)))]
    for copy in cols_in:
        copy.start()
    jobs = (
        (pu, p_hbm, p_cols, ncoarse, ROWS - 3, 3),
        (qu, p2_hbm, p2_cols, ncoarsest, CROWS - 2, 2),
        (pd, p_hbm, p_cols, ncoarse, 0, 3),
        (qd, p2_hbm, p2_cols, ncoarsest, 0, 2),
    )
    copies = [
        pltpu.make_async_copy(src.at[blk(2 * first, 2 * rows)], dst.at[blk(0, 2 * rows)], sems.at[n])
        for n, (dst, src, cols, ncols, first, rows) in enumerate(jobs)
    ]
    for copy in copies:
        copy.start()
    row = lax.broadcasted_iota(jnp.int32, (16, B), 0)
    for copy in cols_in:
        copy.wait()
    for dst, src, cols, ncols, first, rows in jobs:
        flags = jnp.zeros((16, B), F32)
        for r in range(rows):
            side = side_at(cols, first + r, ncols)
            flags = jnp.where(row == 2 * r, (side < 0).astype(F32), flags)
            flags = jnp.where(row == 2 * r + 1, (side > 0).astype(F32), flags)
        dst[pl.ds(2 * rows * B, 16), :] = flags.astype(BF)
    for copy in copies:
        copy.wait()


def bands_of(p_ref, cols, rows, ncoarse):
    out = []
    for r in rows:
        side = side_at(cols, r, ncoarse)
        p0 = p_ref[blk(2 * r), :]
        p1 = p_ref[blk(2 * r + 1), :]
        zero = jnp.zeros_like(p1)
        out.append((jnp.where(side < 0, p1, zero), p0, jnp.where(side > 0, p1, zero)))
    return out


def halo_bands(message, rows):
    flags = message[pl.ds(2 * rows * B, 16), :].astype(F32)
    out = []
    for r in range(rows):
        p0 = message[blk(2 * r), :]
        p1 = message[blk(2 * r + 1), :]
        lower = jnp.broadcast_to(flags[2 * r : 2 * r + 1, :], (B, B)).astype(BF)
        upper = jnp.broadcast_to(flags[2 * r + 1 : 2 * r + 2, :], (B, B)).astype(BF)
        out.append((p1 * lower, p0, p1 * upper))
    return out


def stack_bands(bands):
    return jnp.concatenate([jnp.concatenate(band, axis=1) for band in bands], axis=0)


def shift_at(a_cols, r, k, nfine):
    step = a_cols[k, 0, r] - a_cols[0, 0, r]
    return jnp.where(step > 3, step - nfine, jnp.where(step < -3, step + nfine, step))


def flip(x):
    return jnp.transpose(x, (1, 0))


def is_early():
    return lax.axis_index("gy") % 4 == 0


def group_products(g, a_cols, p_cols, a_ref, p_ref, accs, nfine, ncoarse, store):
    for r in range(4 * g, 4 * g + 4):
        acc = accs[r % len(accs)]
        for s in range(5):
            acc[s] = jnp.zeros((B, B), F32)
        for k in range(K):
            if k == 0:
                v, side, slot0 = r, side_at(p_cols, r, ncoarse), 2
                w0, w1 = p_ref[blk(2 * r), :], p_ref[blk(2 * r + 1), :]
            else:
                v = r + shift_at(a_cols, r, k, nfine)
                inside = jnp.logical_and(v >= 0, v < ROWS)
                v = jnp.clip(v, 0, ROWS - 1)
                side = side_at(p_cols, v, ncoarse)
                slot0 = jnp.where(inside, lax.shift_right_logical(v, 2) - g + 2, 6)
                w0 = p_ref[pl.ds(pl.multiple_of(v * 2 * B, 2 * B), B), :]
                w1 = p_ref[pl.ds(pl.multiple_of(v * 2 * B + B, B), B), :]
            terms = dot(a_ref[blk(r * K + k), :], jnp.concatenate([w0, w1], axis=1))
            acc[slot0] += terms[:, :B]
            acc[slot0 + side] += terms[:, B:]
        for s in range(5):
            store(r, s, acc[s])


def group_rows(g):
    return pl.ds(4 * g * K * B, 4 * K * B)


def start_all(pairs, sems):
    copies = [pltpu.make_async_copy(src, dst, sems.at[n]) for n, (src, dst) in enumerate(pairs)]
    for copy in copies:
        copy.start()
    return copies


def early_kernel(nfine, ncoarse, ac_hbm, pc_hbm, a_hbm, p_hbm, prod, a_cols, p_cols, a_ref, p_ref, sems, *accs):
    @pl.when(is_early())
    def _():
        pairs = [(ac_hbm, a_cols), (pc_hbm, p_cols), (p_hbm, p_ref)]
        pairs += [(a_hbm.at[group_rows(g)], a_ref.at[group_rows(g)]) for g in (0, 3)]
        for copy in start_all(pairs, sems):
            copy.wait()

        def store(r, s, value):
            prod[blk(4 * (r // 12) + r % 4), s * B : (s + 1) * B] = value.astype(BF)

        for g in (0, 3):
            group_products(g, a_cols, p_cols, a_ref, p_ref, accs, nfine, ncoarse, store)


def inner_kernel(
    nfine, ncoarse, ncoarsest, prod_in, ac_hbm, pc_hbm, qc_hbm, a_hbm, p_hbm, p2_hbm,
    prod, part_out, edge_out, wt_out, own_out, ownt_out,
    a_cols, p_cols, p2_cols, a_ref, p_ref, p2_ref, middle, sems, *accs,
):
    pairs = [(ac_hbm, a_cols), (pc_hbm, p_cols), (qc_hbm, p2_cols), (p_hbm, p_ref)]
    pairs += [(a_hbm.at[group_rows(g)], a_ref.at[group_rows(g)]) for g in (0, 3, 1, 2)]
    pairs += [(p2_hbm, p2_ref)]
    copies = start_all(pairs, sems)
    for copy in copies[:6]:
        copy.wait()

    @pl.when(jnp.logical_not(is_early()))
    def _():
        def store(r, s, value):
            prod[blk(4 * (r // 12) + r % 4), s * B : (s + 1) * B] = value.astype(BF)

        for g in (0, 3):
            group_products(g, a_cols, p_cols, a_ref, p_ref, accs, nfine, ncoarse, store)

    for copy in copies[6:]:
        copy.wait()

    def store_middle(r, s, value):
        middle[blk(r - 4), s * B : (s + 1) * B] = value.astype(BF)

    for g in (1, 2):
        group_products(g, a_cols, p_cols, a_ref, p_ref, accs, nfine, ncoarse, store_middle)
    for side in (0, 1):
        first = 0 if side == 0 else ROWS - 3
        for n in range(3):
            r = first + n
            for h in range(3):
                want = (h - 3 if side == 0 else ROWS + h) - r
                at = jnp.int32(0)
                found = jnp.int32(0)
                for k in range(1, K):
                    hit = (shift_at(a_cols, r, k, nfine) == want).astype(jnp.int32)
                    at = at + hit * k
                    found = found + hit
                block = a_ref[pl.ds(pl.multiple_of((r * K + at) * B, B), B), :]
                keep = jnp.where(found > 0, block, jnp.zeros_like(block))
                edge_out[blk(3 * side + n), h * B : (h + 1) * B] = keep if abs(want) <= 3 else jnp.zeros((B, B), BF)
        bands = bands_of(p_ref, p_cols, range(first, first + 3), ncoarse)
        for n in range(3):
            for m in range(3):
                wt_out[blk(3 * side + m), n * B : (n + 1) * B] = flip(bands[n][m])
    own = bands_of(p2_ref, p2_cols, range(CROWS), ncoarsest)
    for n in range(4):
        for m in range(3):
            own_out[blk(n), m * B : (m + 1) * B] = own[n][m]
            ownt_out[blk(m), n * B : (n + 1) * B] = flip(own[n][m])
    part_out[...] = jnp.zeros_like(part_out)
    for g in (1, 2, 0, 3):
        bands = stack_bands(bands_of(p_ref, p_cols, range(4 * g, 4 * g + 4), ncoarse))
        rows = middle[blk(4 * (g - 1), 4), :] if g in (1, 2) else prod[blk(4 * (g // 3), 4), :]
        terms = dot_t(bands, rows)
        for m in range(3):
            at = slice(g * B, (g + 5) * B)
            part_out[g + m, :, at] = part_out[g + m, :, at] + terms[m * B : (m + 1) * B, :]


def middle_kernel(part_in, edge, wt, p_low, p_high, part):
    for side in (0, 1):
        halo = halo_bands(p_high if side else p_low, 3)
        far, tall = (2, 2) if side else (0, 0)
        near = [h for h in range(3) if h != far]
        lanes = slice(0, 2 * B) if side else slice(B, 3 * B)
        terms = dot(edge[blk(3 * side, 3), lanes], stack_bands([halo[h] for h in near]))
        last = dot(edge[blk(3 * side + tall), far * B : (far + 1) * B], stack_bands([halo[far]]))
        extra = jnp.concatenate(
            [(terms[n * B : (n + 1) * B, :] + (last if n == tall else 0.0)).astype(BF) for n in range(3)], axis=0
        )
        terms = dot(wt[blk(3 * side, 3), :], extra)
        for m in range(3):
            j = 3 * side + m
            at = slice(5 * side * B, (5 * side + 3) * B)
            part[j, :, at] = part_in[j, :, at] + terms[m * B : (m + 1) * B, :]


def outer_kernel(part, own, ownt, q_low, q_high, fine_out, mu, md, nu, nd, cp):
    low = halo_bands(q_low, 2)
    high = halo_bands(q_high, 2)
    lines = part[...].astype(BF).reshape(6 * B, 8 * B)
    ta = dot(lines[0 : 4 * B, 0 : 2 * B], stack_bands(low))
    tb = dot(lines[:, 2 * B : 6 * B], own[...])
    tc = dot(lines[2 * B : 6 * B, 6 * B : 8 * B], stack_bands(high))
    for e in range(5):
        for i in range(6):
            pieces = []
            if e < 3 and i < 4:
                pieces.append(ta[i * B : (i + 1) * B, e * B : (e + 1) * B])
            if 1 <= e < 4:
                pieces.append(tb[i * B : (i + 1) * B, (e - 1) * B : e * B])
            if e >= 2 and i >= 2:
                pieces.append(tc[(i - 2) * B : (i - 1) * B, (e - 2) * B : (e - 1) * B])
            value = sum(pieces[1:], pieces[0]) if pieces else jnp.zeros((B, B), F32)
            cp[blk(i), e * B : (e + 1) * B] = value.astype(BF)
    gm = dot_t(stack_bands(low[1:2]), cp[blk(0), 0 : 4 * B])
    g0 = dot(ownt[...], cp[blk(1, 4), :])
    gp = dot_t(stack_bands(high[0:1]), cp[blk(5), B : 5 * B])

    def low_at(m, e):
        return gm[m * B : (m + 1) * B, e * B : (e + 1) * B] if e < 4 else 0.0

    def own_at(m, e):
        return g0[m * B : (m + 1) * B, e * B : (e + 1) * B]

    def high_at(m, e):
        return gp[m * B : (m + 1) * B, (e - 1) * B : e * B] if e > 0 else 0.0

    for e in range(5):
        fine_out[:, e * B : (e + 1) * B] = low_at(2, e) + own_at(1, e) + high_at(0, e)
    to_low = [(low_at(1, e) + own_at(0, e)).astype(BF) for e in range(5)]
    to_high = [(own_at(2, e) + high_at(1, e)).astype(BF) for e in range(5)]
    two_low = [low_at(0, e).astype(BF) for e in range(4)]
    two_high = [high_at(2, e).astype(BF) for e in range(1, 5)]

    def put(dst, coarse_row, q0, fine):
        for t in range(5):
            dst[blk(t), :] = part[coarse_row, :, (q0 + t) * B : (q0 + t + 1) * B].astype(BF)
            dst[blk(5 + t), :] = fine[t]

    def put2(dst, fine):
        for t in range(4):
            dst[blk(t), :] = fine[t]

    put(mu, 5, 3, to_high)
    put(md, 0, 0, to_low)
    put2(nu, two_high)
    put2(nd, two_low)


def column_block(part, j, t):
    q = t + j - 1
    if 0 <= q < 8:
        return part[j + 1, :, q * B : (q + 1) * B]
    return jnp.zeros((B, B), F32)


def store_kernel(part, coarse_hbm, rows, sems):
    copies = []
    for j in range(CROWS):
        for t in range(KC):
            rows[blk(j * KC + t), :] = column_block(part, j, t).astype(BF)
        at = blk(j * KC, KC)
        copies.append(pltpu.make_async_copy(rows.at[at], coarse_hbm.at[at], sems.at[j]))
        copies[-1].start()
    for copy in copies:
        copy.wait()


def last_kernel(coarse_in, part, fine, mu, md, nu, nd, coarse_out, coarsest_out, rows, sems):
    def one(low, t):
        return (mu if low else md)[blk(t), :].astype(F32)

    def two(low, t):
        return (nu if low else nd)[blk(t), :].astype(F32)

    for t in range(KC):
        value = jnp.zeros((B, B), F32)
        if 1 <= t < 6:
            value = value + fine[:, (t - 1) * B : t * B]
        if t < 5:
            value = value + one(True, 5 + t)
        if t >= 2:
            value = value + one(False, 5 + t - 2)
        if t < 4:
            value = value + two(True, t)
        if t >= 3:
            value = value + two(False, t - 3)
        rows[blk(10 + t), :] = value.astype(BF)
    copies = [pltpu.make_async_copy(rows.at[blk(10, KC)], coarsest_out, sems.at[2])]
    copies[0].start()
    for n, j in enumerate((0, 3)):
        for t in range(5):
            rows[blk(5 * n + t), :] = (column_block(part, j, t + 2 * n) + one(n == 0, t)).astype(BF)
        at = blk(j * KC + 2 * n, 5)
        copies.append(pltpu.make_async_copy(rows.at[blk(5 * n, 5)], coarse_out.at[at], sems.at[n]))
        copies[-1].start()
    for copy in copies:
        copy.wait()


def call(kernel, ins, outs, args, scratch=(), cost=None, **kw):
    vmem = pl.BlockSpec(memory_space=pltpu.VMEM)
    hbm = pl.BlockSpec(memory_space=pltpu.HBM)
    kinds = {"v": vmem, "h": hbm}
    aliased = kw.get("input_output_aliases", {})
    args = [
        pltpu.with_memory_space_constraint(x, pltpu.HBM) if c == "h" and n not in aliased else x
        for n, (c, x) in enumerate(zip(ins, args))
    ]
    return pl.pallas_call(
        kernel,
        in_specs=[kinds[c] for c in ins],
        out_specs=tuple(kinds[c] for c, _, _ in outs),
        out_shape=tuple(jax.ShapeDtypeStruct(shape, dtype) for _, shape, dtype in outs),
        scratch_shapes=list(scratch),
        compiler_params=pltpu.CompilerParams(vmem_limit_bytes=40 * 1024 * 1024),
        cost_estimate=cost,
        **kw,
    )(*args)


def body(a_vals, a_cols, p_vals, p_cols, p2_vals, p2_cols):
    devices = lax.axis_size(AXES)
    nfine = ROWS * devices
    ncoarse = CROWS * devices
    a_cols = jnp.transpose(a_cols, (2, 0, 1))
    p_cols = p_cols.reshape(ROWS, 2).T
    p2_cols = p2_cols.reshape(CROWS, 2).T
    a = a_vals.reshape(ROWS * K * B, B)
    p = p_vals.reshape(ROWS * 2 * B, B)
    p2 = p2_vals.reshape(CROWS * 2 * B, B)

    def pack(*refs):
        pack_kernel(ncoarse, devices, *refs)

    pu, qu, pd, qd = call(
        pack,
        "hhhh",
        [("v", (PM, B), BF), ("v", (QM, B), BF), ("v", (PM, B), BF), ("v", (QM, B), BF)],
        (p_cols, p2_cols, p, p2),
        [
            pltpu.SMEM((2, ROWS), jnp.int32),
            pltpu.SMEM((2, CROWS), jnp.int32),
            pltpu.SemaphoreType.DMA((6,)),
        ],
    )
    up = [(i, (i + 1) % devices) for i in range(devices)]
    down = [((i + 1) % devices, i) for i in range(devices)]
    p_low = lax.ppermute(pu, AXES, up)
    q_low = lax.ppermute(qu, AXES, up)

    def early(*refs):
        early_kernel(nfine, ncoarse, *refs)

    (prod,) = call(
        early,
        "hhhh",
        [("v", (8 * B, 5 * B), BF)],
        (a_cols, p_cols, a, p),
        [
            pltpu.SMEM((K, 1, ROWS), jnp.int32),
            pltpu.SMEM((2, ROWS), jnp.int32),
            pltpu.VMEM((ROWS * K * B, B), BF),
            pltpu.VMEM((ROWS * 2 * B, B), BF),
            pltpu.SemaphoreType.DMA((5,)),
            *[pltpu.VMEM((8, B, B), F32) for _ in range(NACC)],
        ],
        pl.CostEstimate(flops=10**6, bytes_accessed=10**6, transcendentals=0),
    )
    p_high = lax.ppermute(pd, AXES, down)
    q_high = lax.ppermute(qd, AXES, down)

    def inner(*refs):
        inner_kernel(nfine, ncoarse, devices, *refs)

    prod, part, edge, wt, own, ownt = call(
        inner,
        "vhhhhhh",
        [
            ("v", (8 * B, 5 * B), BF),
            ("v", (6, B, 8 * B), F32),
            ("v", (6 * B, 3 * B), BF),
            ("v", (6 * B, 3 * B), BF),
            ("v", (4 * B, 3 * B), BF),
            ("v", (3 * B, 4 * B), BF),
        ],
        (prod, a_cols, p_cols, p2_cols, a, p, p2),
        [
            pltpu.SMEM((K, 1, ROWS), jnp.int32),
            pltpu.SMEM((2, ROWS), jnp.int32),
            pltpu.SMEM((2, CROWS), jnp.int32),
            pltpu.VMEM((ROWS * K * B, B), BF),
            pltpu.VMEM((ROWS * 2 * B, B), BF),
            pltpu.VMEM((CROWS * 2 * B, B), BF),
            pltpu.VMEM((8 * B, 5 * B), BF),
            pltpu.SemaphoreType.DMA((9,)),
            *[pltpu.VMEM((8, B, B), F32) for _ in range(NACC)],
        ],
        pl.CostEstimate(flops=10**9, bytes_accessed=8 * 10**6, transcendentals=0),
        input_output_aliases={0: 0},
    )
    (part,) = call(
        middle_kernel,
        "vvvvv",
        [("v", (6, B, 8 * B), F32)],
        (part, edge, wt, p_low, p_high),
        cost=pl.CostEstimate(flops=10**9, bytes_accessed=4 * 10**6, transcendentals=0),
        input_output_aliases={0: 0},
    )
    fine, mu, md, nu, nd = call(
        outer_kernel,
        "vvvvv",
        [
            ("v", (B, 5 * B), F32),
            ("v", (10 * B, B), BF),
            ("v", (10 * B, B), BF),
            ("v", (4 * B, B), BF),
            ("v", (4 * B, B), BF),
        ],
        (part, own, ownt, q_low, q_high),
        [pltpu.VMEM((6 * B, 5 * B), BF)],
        pl.CostEstimate(flops=10**9, bytes_accessed=4 * 10**6, transcendentals=0),
    )
    up2 = [(i, (i + 2) % devices) for i in range(devices)]
    down2 = [((i + 2) % devices, i) for i in range(devices)]
    mu = lax.ppermute(mu, AXES, up)
    nu = lax.ppermute(nu, AXES, up2)
    md = lax.ppermute(md, AXES, down)
    nd = lax.ppermute(nd, AXES, down2)
    (coarse,) = call(
        store_kernel,
        "v",
        [("h", (CROWS * KC * B, B), BF)],
        (part,),
        [pltpu.VMEM((CROWS * KC * B, B), BF), pltpu.SemaphoreType.DMA((CROWS,))],
        pl.CostEstimate(flops=10**6, bytes_accessed=3 * 10**6, transcendentals=0),
    )
    coarse, coarsest = call(
        last_kernel,
        "hvvvvvv",
        [("h", (CROWS * KC * B, B), BF), ("h", (KC * B, B), BF)],
        (coarse, part, fine, mu, md, nu, nd),
        [pltpu.VMEM(((10 + KC) * B, B), BF), pltpu.SemaphoreType.DMA((3,))],
        input_output_aliases={0: 0},
    )
    return coarse.reshape(1, CROWS, KC, B, B), coarsest.reshape(1, 1, KC, B, B)


def solution(mesh):
    blocks = P(None, AXES, None, None, None)
    cols = P(None, AXES, None)

    return jax.shard_map(
        body,
        mesh=mesh,
        in_specs=(blocks, cols, blocks, cols, blocks, cols),
        out_specs=(blocks, blocks),
        check_vma=False,
    )
```

```python
import jax
import jax.numpy as jnp
from jax import lax
from jax.experimental import pallas as pl
from jax.experimental.pallas import tpu as pltpu
from jax.sharding import PartitionSpec as P


B = 128
K = 5
KC = 7
ROWS = 16
CROWS = 4
BF = jnp.bfloat16
F32 = jnp.float32
PM = 6 * B + 16
QM = 4 * B + 16
NACC = 8
AXES = ("gx", "gy")


def blk(i, n=1):
    return pl.ds(i * B, n * B)


def side_at(cols, r, ncoarse):
    step = cols[1, r] - cols[0, r]
    return jnp.where(jnp.logical_or(step == 1, step == 1 - ncoarse), 1, -1)


def dot(a, b):
    return jnp.dot(a, b, preferred_element_type=F32)


def dot_t(a, b):
    return lax.dot_general(a, b, (((0,), (0,)), ((), ())), preferred_element_type=F32)


def pack_kernel(ncoarse, ncoarsest, pc_hbm, qc_hbm, p_hbm, p2_hbm, pu, qu, pd, qd, p_cols, p2_cols, sems):
    cols_in = [pltpu.make_async_copy(x, y, sems.at[4 + n]) for n, (x, y) in enumerate(((pc_hbm, p_cols), (qc_hbm, p2_cols)))]
    for copy in cols_in:
        copy.start()
    jobs = (
        (pu, p_hbm, p_cols, ncoarse, ROWS - 3, 3),
        (qu, p2_hbm, p2_cols, ncoarsest, CROWS - 2, 2),
        (pd, p_hbm, p_cols, ncoarse, 0, 3),
        (qd, p2_hbm, p2_cols, ncoarsest, 0, 2),
    )
    copies = [
        pltpu.make_async_copy(src.at[blk(2 * first, 2 * rows)], dst.at[blk(0, 2 * rows)], sems.at[n])
        for n, (dst, src, cols, ncols, first, rows) in enumerate(jobs)
    ]
    for copy in copies:
        copy.start()
    row = lax.broadcasted_iota(jnp.int32, (16, B), 0)
    for copy in cols_in:
        copy.wait()
    for dst, src, cols, ncols, first, rows in jobs:
        flags = jnp.zeros((16, B), F32)
        for r in range(rows):
            side = side_at(cols, first + r, ncols)
            flags = jnp.where(row == 2 * r, (side < 0).astype(F32), flags)
            flags = jnp.where(row == 2 * r + 1, (side > 0).astype(F32), flags)
        dst[pl.ds(2 * rows * B, 16), :] = flags.astype(BF)
    for copy in copies:
        copy.wait()


def bands_of(p_ref, cols, rows, ncoarse):
    out = []
    for r in rows:
        side = side_at(cols, r, ncoarse)
        p0 = p_ref[blk(2 * r), :]
        p1 = p_ref[blk(2 * r + 1), :]
        zero = jnp.zeros_like(p1)
        out.append((jnp.where(side < 0, p1, zero), p0, jnp.where(side > 0, p1, zero)))
    return out


def halo_bands(message, rows):
    flags = message[pl.ds(2 * rows * B, 16), :].astype(F32)
    out = []
    for r in range(rows):
        p0 = message[blk(2 * r), :]
        p1 = message[blk(2 * r + 1), :]
        lower = jnp.broadcast_to(flags[2 * r : 2 * r + 1, :], (B, B)).astype(BF)
        upper = jnp.broadcast_to(flags[2 * r + 1 : 2 * r + 2, :], (B, B)).astype(BF)
        out.append((p1 * lower, p0, p1 * upper))
    return out


def stack_bands(bands):
    return jnp.concatenate([jnp.concatenate(band, axis=1) for band in bands], axis=0)


def shift_at(a_cols, r, k, nfine):
    step = a_cols[k, 0, r] - a_cols[0, 0, r]
    return jnp.where(step > 3, step - nfine, jnp.where(step < -3, step + nfine, step))


def flip(x):
    return jnp.transpose(x, (1, 0))


def is_early():
    return lax.axis_index("gy") % 4 == 0


def is_first():
    return jnp.logical_and(lax.axis_index("gx") < 2, lax.axis_index("gy") == 0)


def group_products(g, a_cols, p_cols, a_ref, p_ref, accs, nfine, ncoarse, store):
    for r in range(4 * g, 4 * g + 4):
        acc = accs[r % len(accs)]
        for s in range(5):
            acc[s] = jnp.zeros((B, B), F32)
        for k in range(K):
            if k == 0:
                v, side, slot0 = r, side_at(p_cols, r, ncoarse), 2
                w0, w1 = p_ref[blk(2 * r), :], p_ref[blk(2 * r + 1), :]
            else:
                v = r + shift_at(a_cols, r, k, nfine)
                inside = jnp.logical_and(v >= 0, v < ROWS)
                v = jnp.clip(v, 0, ROWS - 1)
                side = side_at(p_cols, v, ncoarse)
                slot0 = jnp.where(inside, lax.shift_right_logical(v, 2) - g + 2, 6)
                w0 = p_ref[pl.ds(pl.multiple_of(v * 2 * B, 2 * B), B), :]
                w1 = p_ref[pl.ds(pl.multiple_of(v * 2 * B + B, B), B), :]
            terms = dot(a_ref[blk(r * K + k), :], jnp.concatenate([w0, w1], axis=1))
            acc[slot0] += terms[:, :B]
            acc[slot0 + side] += terms[:, B:]
        for s in range(5):
            store(r, s, acc[s])


def group_rows(g):
    return pl.ds(4 * g * K * B, 4 * K * B)


def start_all(pairs, sems):
    copies = [pltpu.make_async_copy(src, dst, sems.at[n]) for n, (src, dst) in enumerate(pairs)]
    for copy in copies:
        copy.start()
    return copies


def early_kernel(nfine, ncoarse, ac_hbm, pc_hbm, a_hbm, p_hbm, prod, a_cols, p_cols, a_ref, p_ref, sems, *accs):
    @pl.when(is_early())
    def _():
        pairs = [(ac_hbm, a_cols), (pc_hbm, p_cols), (p_hbm, p_ref)]
        pairs += [(a_hbm.at[group_rows(g)], a_ref.at[group_rows(g)]) for g in (0, 3)]
        for copy in start_all(pairs, sems):
            copy.wait()

        def store(r, s, value):
            prod[blk(r), s * B : (s + 1) * B] = value.astype(BF)

        for g in (0, 3):
            group_products(g, a_cols, p_cols, a_ref, p_ref, accs, nfine, ncoarse, store)

        @pl.when(is_first())
        def _():
            pairs = [(a_hbm.at[group_rows(g)], a_ref.at[group_rows(g)]) for g in (1, 2)]
            for copy in start_all(pairs, sems):
                copy.wait()
            for g in (1, 2):
                group_products(g, a_cols, p_cols, a_ref, p_ref, accs, nfine, ncoarse, store)


def inner_kernel(
    nfine, ncoarse, ncoarsest, prod_in, ac_hbm, pc_hbm, qc_hbm, a_hbm, p_hbm, p2_hbm,
    prod, part_out, edge_out, wt_out, own_out, ownt_out,
    a_cols, p_cols, p2_cols, a_ref, p_ref, p2_ref, sems, *accs,
):
    pairs = [(ac_hbm, a_cols), (pc_hbm, p_cols), (qc_hbm, p2_cols), (p_hbm, p_ref)]
    pairs += [(a_hbm.at[group_rows(g)], a_ref.at[group_rows(g)]) for g in (0, 3, 1, 2)]
    pairs += [(p2_hbm, p2_ref)]
    copies = start_all(pairs, sems)
    for copy in copies[:6]:
        copy.wait()

    @pl.when(jnp.logical_not(is_early()))
    def _():
        def store(r, s, value):
            prod[blk(r), s * B : (s + 1) * B] = value.astype(BF)

        for g in (0, 3):
            group_products(g, a_cols, p_cols, a_ref, p_ref, accs, nfine, ncoarse, store)

    for copy in copies[6:]:
        copy.wait()

    @pl.when(jnp.logical_not(is_first()))
    def _():
        def store(r, s, value):
            prod[blk(r), s * B : (s + 1) * B] = value.astype(BF)

        for g in (1, 2):
            group_products(g, a_cols, p_cols, a_ref, p_ref, accs, nfine, ncoarse, store)

    for side in (0, 1):
        first = 0 if side == 0 else ROWS - 3
        for n in range(3):
            r = first + n
            for h in range(3):
                want = (h - 3 if side == 0 else ROWS + h) - r
                at = jnp.int32(0)
                found = jnp.int32(0)
                for k in range(1, K):
                    hit = (shift_at(a_cols, r, k, nfine) == want).astype(jnp.int32)
                    at = at + hit * k
                    found = found + hit
                block = a_ref[pl.ds(pl.multiple_of((r * K + at) * B, B), B), :]
                keep = jnp.where(found > 0, block, jnp.zeros_like(block))
                edge_out[blk(3 * side + n), h * B : (h + 1) * B] = keep if abs(want) <= 3 else jnp.zeros((B, B), BF)
        bands = bands_of(p_ref, p_cols, range(first, first + 3), ncoarse)
        for n in range(3):
            for m in range(3):
                wt_out[blk(3 * side + m), n * B : (n + 1) * B] = flip(bands[n][m])
    own = bands_of(p2_ref, p2_cols, range(CROWS), ncoarsest)
    for n in range(4):
        for m in range(3):
            own_out[blk(n), m * B : (m + 1) * B] = own[n][m]
            ownt_out[blk(m), n * B : (n + 1) * B] = flip(own[n][m])
    part_out[...] = jnp.zeros_like(part_out)
    for g in (1, 2, 0, 3):
        bands = stack_bands(bands_of(p_ref, p_cols, range(4 * g, 4 * g + 4), ncoarse))
        terms = dot_t(bands, prod[blk(4 * g, 4), :])
        for m in range(3):
            at = slice(g * B, (g + 5) * B)
            part_out[g + m, :, at] = part_out[g + m, :, at] + terms[m * B : (m + 1) * B, :]


def middle_kernel(part_in, edge, wt, p_low, p_high, part):
    for side in (0, 1):
        halo = halo_bands(p_high if side else p_low, 3)
        far, tall = (2, 2) if side else (0, 0)
        near = [h for h in range(3) if h != far]
        lanes = slice(0, 2 * B) if side else slice(B, 3 * B)
        terms = dot(edge[blk(3 * side, 3), lanes], stack_bands([halo[h] for h in near]))
        last = dot(edge[blk(3 * side + tall), far * B : (far + 1) * B], stack_bands([halo[far]]))
        extra = jnp.concatenate(
            [(terms[n * B : (n + 1) * B, :] + (last if n == tall else 0.0)).astype(BF) for n in range(3)], axis=0
        )
        terms = dot(wt[blk(3 * side, 3), :], extra)
        for m in range(3):
            j = 3 * side + m
            at = slice(5 * side * B, (5 * side + 3) * B)
            part[j, :, at] = part_in[j, :, at] + terms[m * B : (m + 1) * B, :]


def outer_kernel(part, own, ownt, q_low, q_high, fine_out, mu, md, nu, nd, cp):
    low = halo_bands(q_low, 2)
    high = halo_bands(q_high, 2)
    lines = part[...].astype(BF).reshape(6 * B, 8 * B)
    ta = dot(lines[0 : 4 * B, 0 : 2 * B], stack_bands(low))
    tb = dot(lines[:, 2 * B : 6 * B], own[...])
    tc = dot(lines[2 * B : 6 * B, 6 * B : 8 * B], stack_bands(high))
    for e in range(5):
        for i in range(6):
            pieces = []
            if e < 3 and i < 4:
                pieces.append(ta[i * B : (i + 1) * B, e * B : (e + 1) * B])
            if 1 <= e < 4:
                pieces.append(tb[i * B : (i + 1) * B, (e - 1) * B : e * B])
            if e >= 2 and i >= 2:
                pieces.append(tc[(i - 2) * B : (i - 1) * B, (e - 2) * B : (e - 1) * B])
            value = sum(pieces[1:], pieces[0]) if pieces else jnp.zeros((B, B), F32)
            cp[blk(i), e * B : (e + 1) * B] = value.astype(BF)
    gm = dot_t(stack_bands(low[1:2]), cp[blk(0), 0 : 4 * B])
    g0 = dot(ownt[...], cp[blk(1, 4), :])
    gp = dot_t(stack_bands(high[0:1]), cp[blk(5), B : 5 * B])

    def low_at(m, e):
        return gm[m * B : (m + 1) * B, e * B : (e + 1) * B] if e < 4 else 0.0

    def own_at(m, e):
        return g0[m * B : (m + 1) * B, e * B : (e + 1) * B]

    def high_at(m, e):
        return gp[m * B : (m + 1) * B, (e - 1) * B : e * B] if e > 0 else 0.0

    for e in range(5):
        fine_out[:, e * B : (e + 1) * B] = low_at(2, e) + own_at(1, e) + high_at(0, e)
    to_low = [(low_at(1, e) + own_at(0, e)).astype(BF) for e in range(5)]
    to_high = [(own_at(2, e) + high_at(1, e)).astype(BF) for e in range(5)]
    two_low = [low_at(0, e).astype(BF) for e in range(4)]
    two_high = [high_at(2, e).astype(BF) for e in range(1, 5)]

    def put(dst, coarse_row, q0, fine):
        for t in range(5):
            dst[blk(t), :] = part[coarse_row, :, (q0 + t) * B : (q0 + t + 1) * B].astype(BF)
            dst[blk(5 + t), :] = fine[t]

    def put2(dst, fine):
        for t in range(4):
            dst[blk(t), :] = fine[t]

    put(mu, 5, 3, to_high)
    put(md, 0, 0, to_low)
    put2(nu, two_high)
    put2(nd, two_low)


def column_block(part, j, t):
    q = t + j - 1
    if 0 <= q < 8:
        return part[j + 1, :, q * B : (q + 1) * B]
    return jnp.zeros((B, B), F32)


def store_kernel(part, coarse_hbm, rows, sems):
    copies = []
    for j in range(CROWS):
        for t in range(KC):
            rows[blk(j * KC + t), :] = column_block(part, j, t).astype(BF)
        at = blk(j * KC, KC)
        copies.append(pltpu.make_async_copy(rows.at[at], coarse_hbm.at[at], sems.at[j]))
        copies[-1].start()
    for copy in copies:
        copy.wait()


def last_kernel(coarse_in, part, fine, mu, md, nu, nd, coarse_out, coarsest_out, rows, sems):
    def one(low, t):
        return (mu if low else md)[blk(t), :].astype(F32)

    def two(low, t):
        return (nu if low else nd)[blk(t), :].astype(F32)

    for t in range(KC):
        value = jnp.zeros((B, B), F32)
        if 1 <= t < 6:
            value = value + fine[:, (t - 1) * B : t * B]
        if t < 5:
            value = value + one(True, 5 + t)
        if t >= 2:
            value = value + one(False, 5 + t - 2)
        if t < 4:
            value = value + two(True, t)
        if t >= 3:
            value = value + two(False, t - 3)
        rows[blk(10 + t), :] = value.astype(BF)
    copies = [pltpu.make_async_copy(rows.at[blk(10, KC)], coarsest_out, sems.at[2])]
    copies[0].start()
    for n, j in enumerate((0, 3)):
        for t in range(5):
            rows[blk(5 * n + t), :] = (column_block(part, j, t + 2 * n) + one(n == 0, t)).astype(BF)
        at = blk(j * KC + 2 * n, 5)
        copies.append(pltpu.make_async_copy(rows.at[blk(5 * n, 5)], coarse_out.at[at], sems.at[n]))
        copies[-1].start()
    for copy in copies:
        copy.wait()


def call(kernel, ins, outs, args, scratch=(), cost=None, **kw):
    vmem = pl.BlockSpec(memory_space=pltpu.VMEM)
    hbm = pl.BlockSpec(memory_space=pltpu.HBM)
    kinds = {"v": vmem, "h": hbm}
    aliased = kw.get("input_output_aliases", {})
    args = [
        pltpu.with_memory_space_constraint(x, pltpu.HBM) if c == "h" and n not in aliased else x
        for n, (c, x) in enumerate(zip(ins, args))
    ]
    return pl.pallas_call(
        kernel,
        in_specs=[kinds[c] for c in ins],
        out_specs=tuple(kinds[c] for c, _, _ in outs),
        out_shape=tuple(jax.ShapeDtypeStruct(shape, dtype) for _, shape, dtype in outs),
        scratch_shapes=list(scratch),
        compiler_params=pltpu.CompilerParams(vmem_limit_bytes=40 * 1024 * 1024),
        cost_estimate=cost,
        **kw,
    )(*args)


def body(a_vals, a_cols, p_vals, p_cols, p2_vals, p2_cols):
    devices = lax.axis_size(AXES)
    nfine = ROWS * devices
    ncoarse = CROWS * devices
    a_cols = jnp.transpose(a_cols, (2, 0, 1))
    p_cols = p_cols.reshape(ROWS, 2).T
    p2_cols = p2_cols.reshape(CROWS, 2).T
    a = a_vals.reshape(ROWS * K * B, B)
    p = p_vals.reshape(ROWS * 2 * B, B)
    p2 = p2_vals.reshape(CROWS * 2 * B, B)

    def pack(*refs):
        pack_kernel(ncoarse, devices, *refs)

    pu, qu, pd, qd = call(
        pack,
        "hhhh",
        [("v", (PM, B), BF), ("v", (QM, B), BF), ("v", (PM, B), BF), ("v", (QM, B), BF)],
        (p_cols, p2_cols, p, p2),
        [
            pltpu.SMEM((2, ROWS), jnp.int32),
            pltpu.SMEM((2, CROWS), jnp.int32),
            pltpu.SemaphoreType.DMA((6,)),
        ],
    )
    up = [(i, (i + 1) % devices) for i in range(devices)]
    down = [((i + 1) % devices, i) for i in range(devices)]
    p_low = lax.ppermute(pu, AXES, up)
    q_low = lax.ppermute(qu, AXES, up)

    def early(*refs):
        early_kernel(nfine, ncoarse, *refs)

    (prod,) = call(
        early,
        "hhhh",
        [("v", (ROWS * B, 5 * B), BF)],
        (a_cols, p_cols, a, p),
        [
            pltpu.SMEM((K, 1, ROWS), jnp.int32),
            pltpu.SMEM((2, ROWS), jnp.int32),
            pltpu.VMEM((ROWS * K * B, B), BF),
            pltpu.VMEM((ROWS * 2 * B, B), BF),
            pltpu.SemaphoreType.DMA((5,)),
            *[pltpu.VMEM((8, B, B), F32) for _ in range(NACC)],
        ],
        pl.CostEstimate(flops=10**6, bytes_accessed=10**6, transcendentals=0),
    )
    p_high = lax.ppermute(pd, AXES, down)
    q_high = lax.ppermute(qd, AXES, down)

    def inner(*refs):
        inner_kernel(nfine, ncoarse, devices, *refs)

    prod, part, edge, wt, own, ownt = call(
        inner,
        "vhhhhhh",
        [
            ("v", (ROWS * B, 5 * B), BF),
            ("v", (6, B, 8 * B), F32),
            ("v", (6 * B, 3 * B), BF),
            ("v", (6 * B, 3 * B), BF),
            ("v", (4 * B, 3 * B), BF),
            ("v", (3 * B, 4 * B), BF),
        ],
        (prod, a_cols, p_cols, p2_cols, a, p, p2),
        [
            pltpu.SMEM((K, 1, ROWS), jnp.int32),
            pltpu.SMEM((2, ROWS), jnp.int32),
            pltpu.SMEM((2, CROWS), jnp.int32),
            pltpu.VMEM((ROWS * K * B, B), BF),
            pltpu.VMEM((ROWS * 2 * B, B), BF),
            pltpu.VMEM((CROWS * 2 * B, B), BF),
            pltpu.SemaphoreType.DMA((9,)),
            *[pltpu.VMEM((8, B, B), F32) for _ in range(NACC)],
        ],
        pl.CostEstimate(flops=10**9, bytes_accessed=8 * 10**6, transcendentals=0),
        input_output_aliases={0: 0},
    )
    (part,) = call(
        middle_kernel,
        "vvvvv",
        [("v", (6, B, 8 * B), F32)],
        (part, edge, wt, p_low, p_high),
        cost=pl.CostEstimate(flops=10**9, bytes_accessed=4 * 10**6, transcendentals=0),
        input_output_aliases={0: 0},
    )
    fine, mu, md, nu, nd = call(
        outer_kernel,
        "vvvvv",
        [
            ("v", (B, 5 * B), F32),
            ("v", (10 * B, B), BF),
            ("v", (10 * B, B), BF),
            ("v", (4 * B, B), BF),
            ("v", (4 * B, B), BF),
        ],
        (part, own, ownt, q_low, q_high),
        [pltpu.VMEM((6 * B, 5 * B), BF)],
        pl.CostEstimate(flops=10**9, bytes_accessed=4 * 10**6, transcendentals=0),
    )
    up2 = [(i, (i + 2) % devices) for i in range(devices)]
    down2 = [((i + 2) % devices, i) for i in range(devices)]
    mu = lax.ppermute(mu, AXES, up)
    nu = lax.ppermute(nu, AXES, up2)
    md = lax.ppermute(md, AXES, down)
    nd = lax.ppermute(nd, AXES, down2)
    (coarse,) = call(
        store_kernel,
        "v",
        [("h", (CROWS * KC * B, B), BF)],
        (part,),
        [pltpu.VMEM((CROWS * KC * B, B), BF), pltpu.SemaphoreType.DMA((CROWS,))],
        pl.CostEstimate(flops=10**6, bytes_accessed=3 * 10**6, transcendentals=0),
    )
    coarse, coarsest = call(
        last_kernel,
        "hvvvvvv",
        [("h", (CROWS * KC * B, B), BF), ("h", (KC * B, B), BF)],
        (coarse, part, fine, mu, md, nu, nd),
        [pltpu.VMEM(((10 + KC) * B, B), BF), pltpu.SemaphoreType.DMA((3,))],
        input_output_aliases={0: 0},
    )
    return coarse.reshape(1, CROWS, KC, B, B), coarsest.reshape(1, 1, KC, B, B)


def solution(mesh):
    blocks = P(None, AXES, None, None, None)
    cols = P(None, AXES, None)

    return jax.shard_map(
        body,
        mesh=mesh,
        in_specs=(blocks, cols, blocks, cols, blocks, cols),
        out_specs=(blocks, blocks),
        check_vma=False,
    )
```
